128 devices in a mesh: lat: 8 (over z_hi, x), lon: 16 (over y, z_lo, core).
Axes of the slice: x: 4, y: 4, z: 4 (z_hi: 2, z_lo: 2; z = z_hi * 2 + z_lo), core: 2. Of those that a mesh axis runs over, the one named last changes fastest.
Arguments:
- features: bfloat16 [128, 3072, 128], P('lat', 'lon'), may hold values from -6 to 6
- cotangent: bfloat16 [128, 3072, 128], P('lat', 'lon'), may hold values from -6 to 6
- w_first: bfloat16 [1152, 128], P(('lat', 'lon')), may hold values from -0.1875 to 0.1875
- w_second: bfloat16 [1152, 128], P(('lat', 'lon')), may hold values from -0.1875 to 0.1875
Outputs:
- grad_features: bfloat16 [128, 3072, 128], P('lat', 'lon')
- grad_first: float32 [1152, 128], P(('lat', 'lon'))
- grad_second: float32 [1152, 128], P(('lat', 'lon'))
The draws below stay inside these ranges and needn't reach their ends.
All inputs are finite; a program needn't handle non-finite values.
Results may differ from the reference program's by a relative error of at most 0.0033.
Values may be sent and summed in bfloat16 or wider, within the bound.
No kernel may reach another device: no remote copies, remote signals or barrier semaphores. Data moves between devices by JAX's collectives and lax.ppermute only.
A program may use at most 64 MiB of HBM per device.

```python
import jax
import jax.numpy as jnp
from jax import lax

CH = 128
NLAT = 128
NLON = 3072
TAPS = 1152


def steps_of(rng, shape, shards, smallest, top_value):
    def one(axis_at, shards_of):
        heights = jax.random.uniform(jax.random.fold_in(jax.random.fold_in(rng, 6), axis_at), (shards_of,), jnp.float32, smallest / len(shards), top_value / len(shards))
        return jnp.repeat(jnp.exp(heights), shape[axis_at] // shards_of).reshape((-1,) + (1,) * (len(shape) - axis_at - 1))

    gain = one(*shards[0])
    for cut in shards[1:]:
        gain = gain * one(*cut)
    return gain


def centred(stream_key, dims, spread, limit, pieces=(), kind=jnp.bfloat16):
    drawn = spread * jax.random.normal(stream_key, dims, jnp.float32)
    if pieces:
        drawn = drawn * steps_of(stream_key, dims, pieces, -0.22, 0.18)
    return jnp.clip(drawn, -limit, limit).astype(kind)


def setup_inputs(seed: int = 0) -> dict:
    seeds = jax.random.split(jax.random.key(seed), 5)
    features = centred(seeds[0], (NLAT, NLON, CH), 1.0, 6.0, ((0, 8), (1, 16)))
    cotangent = centred(seeds[1], (NLAT, NLON, CH), 1.0, 6.0, ((0, 8), (1, 16)))
    w_first = centred(seeds[2], (TAPS, CH), TAPS ** -0.5, 0.1875, ((0, 128),))
    w_second = centred(seeds[3], (TAPS, CH), TAPS ** -0.5, 0.1875, ((0, 128),))
    return {"features": features, "cotangent": cotangent, "w_first": w_first, "w_second": w_second}


def pad_field(field, width):
    field = jnp.concatenate([field[:, -width:], field, field[:, :width]], 1)
    return jnp.pad(field, ((width, width), (0, 0), (0, 0)))

def forward_conv(padded, weight, rows, cols):
    chans = padded.shape[2]
    total = jnp.zeros((rows * cols, weight.shape[1]), jnp.float32)
    for tap in range(9):
        shift_r, shift_c = divmod(tap, 3)
        piece = padded[shift_r:shift_r + rows, shift_c:shift_c + cols].reshape(-1, chans)
        total = total + jnp.dot(piece, weight[tap * chans:(tap + 1) * chans], preferred_element_type=jnp.float32)
    return total.reshape(rows, cols, -1)

def transpose_conv(padded, weight, rows, cols):
    chans = weight.shape[1]
    inner = weight.shape[0] // 9
    total = jnp.zeros((rows * cols, inner), jnp.float32)
    for tap in range(9):
        shift_r, shift_c = divmod(tap, 3)
        piece = padded[2 - shift_r:2 - shift_r + rows, 2 - shift_c:2 - shift_c + cols].reshape(-1, chans)
        block = weight[tap * inner:(tap + 1) * inner]
        total = total + lax.dot_general(piece, block, (((1,), (1,)), ((), ())), preferred_element_type=jnp.float32)
    return total.reshape(rows, cols, -1)

def weight_grad(padded, grad_out, rows, cols):
    chans = padded.shape[2]
    flat_grad = grad_out.reshape(-1, grad_out.shape[2])
    blocks = []
    for tap in range(9):
        shift_r, shift_c = divmod(tap, 3)
        piece = padded[shift_r:shift_r + rows, shift_c:shift_c + cols].reshape(-1, chans)
        blocks.append(lax.dot_general(piece, flat_grad, (((0,), (0,)), ((), ())), preferred_element_type=jnp.float32))
    return jnp.concatenate(blocks, 0)

def reference(features, cotangent, w_first, w_second):
    rows, cols = (features.shape[0], features.shape[1])
    feat_pad = pad_field(features, 1)
    pre = forward_conv(feat_pad, w_first, rows, cols)
    act = jax.nn.silu(pre).astype(jnp.bfloat16)
    grad_second = weight_grad(pad_field(act, 1), cotangent, rows, cols)
    back_act = transpose_conv(pad_field(cotangent, 1), w_second, rows, cols)
    sigma = jax.nn.sigmoid(pre)
    back_pre = (back_act * sigma * (1.0 + pre * (1.0 - sigma))).astype(jnp.bfloat16)
    grad_first = weight_grad(feat_pad, back_pre, rows, cols)
    grad_features = (cotangent.astype(jnp.float32) + transpose_conv(pad_field(back_pre, 1), w_first, rows, cols)).astype(jnp.bfloat16)
    return (grad_features, grad_first, grad_second)
```

```python
import jax
import jax.numpy as jnp
from jax import lax
from jax.sharding import PartitionSpec as P

AXES = ("lat", "lon")


def ring(axis, step, periodic):
    count = lax.axis_size(axis)
    pairs = [(i, (i + step) % count) for i in range(count)]
    if not periodic:
        pairs = [(i, j) for i, j in pairs if j == i + step]
    return pairs


def add_rims(fields, width):
    low = lax.ppermute(fields[:, :, -width:], "lon", ring("lon", 1, True))
    high = lax.ppermute(fields[:, :, :width], "lon", ring("lon", -1, True))
    fields = jnp.concatenate([low, fields, high], axis=2)
    low = lax.ppermute(fields[:, -width:], "lat", ring("lat", 1, False))
    high = lax.ppermute(fields[:, :width], "lat", ring("lat", -1, False))
    return jnp.concatenate([low, fields, high], axis=1)


def gather_kernels(w_first, w_second):
    count = lax.axis_size(AXES)
    rows, chans = w_first.shape
    mine = jnp.concatenate([w_first, w_second], 0).reshape(1, rows, 2, chans)
    sent = jnp.broadcast_to(mine, (count, rows, 2, chans))
    got = lax.all_to_all(sent, AXES, 0, 0, tiled=True).reshape(count, 2, rows, chans)
    return got[:, 0].reshape(-1, chans), got[:, 1].reshape(-1, chans)


def scatter_sums(first, second):
    count = lax.axis_size(AXES)
    chans = first.shape[1]
    rows = first.shape[0] // count
    core = lax.axis_index(AXES) % 2
    both = jnp.concatenate(
        [first.reshape(count, rows, chans), second.reshape(count, rows, chans)], 1
    ).reshape(count // 2, 2, rows * 2, chans)
    keep = jnp.where(core == 0, both[:, 0], both[:, 1])
    send = jnp.where(core == 0, both[:, 1], both[:, 0])
    got = lax.ppermute(send, AXES, [(i, i ^ 1) for i in range(count)])
    part = (keep + got).reshape(count // 2, rows, 2, chans)
    groups = [list(range(parity, count, 2)) for parity in range(2)]
    parts = lax.all_to_all(part, AXES, 0, 0, tiled=True, axis_index_groups=groups)
    total = parts.sum(0).reshape(2, rows, chans)
    return total[0], total[1]


def local(features, cotangent, w_first, w_second):
    rows, cols, chans = features.shape
    kernel_one, kernel_two = gather_kernels(w_first, w_second)
    fields = add_rims(jnp.stack([features, cotangent]), 2)
    feat_pad, grad_pad = fields[0], fields[1]

    def conv(padded, weight, flip, height, width):
        total = jnp.zeros((height * width, chans), jnp.float32)
        for tap in range(9):
            a, b = divmod(tap, 3)
            if flip:
                a, b = 2 - a, 2 - b
            piece = padded[a : a + height, b : b + width].reshape(-1, chans)
            block = weight[tap * chans : (tap + 1) * chans]
            total = total + lax.dot_general(
                piece,
                block,
                (((1,), (1 if flip else 0,)), ((), ())),
                preferred_element_type=jnp.float32,
            )
        return total.reshape(height, width, chans)

    pre = conv(feat_pad, kernel_one, False, rows + 2, cols + 2)
    back_act = conv(grad_pad, kernel_two, True, rows + 2, cols + 2)
    sigma = jax.nn.sigmoid(pre)
    act = (pre * sigma).astype(jnp.bfloat16)[1:-1, 1:-1].reshape(-1, chans)
    back_pre = back_act * sigma * (1.0 + pre * (1.0 - sigma))
    place = lax.axis_index("lat") * rows - 1 + lax.broadcasted_iota(
        jnp.int32, (rows + 2, 1, 1), 0
    )
    inside = (place >= 0) & (place < rows * lax.axis_size("lat"))
    back_pre = jnp.where(inside, back_pre, 0.0).astype(jnp.bfloat16)
    back_own = back_pre[1:-1, 1:-1].reshape(-1, chans)
    firsts, seconds = [], []
    for tap in range(9):
        a, b = divmod(tap, 3)
        piece = feat_pad[a + 1 : a + 1 + rows, b + 1 : b + 1 + cols].reshape(-1, chans)
        firsts.append(
            lax.dot_general(
                piece, back_own, (((0,), (0,)), ((), ())), preferred_element_type=jnp.float32
            )
        )
        piece = grad_pad[3 - a : 3 - a + rows, 3 - b : 3 - b + cols].reshape(-1, chans)
        seconds.append(
            lax.dot_general(
                act, piece, (((0,), (0,)), ((), ())), preferred_element_type=jnp.float32
            )
        )
    grad_first, grad_second = scatter_sums(
        jnp.concatenate(firsts, 0), jnp.concatenate(seconds, 0)
    )
    grad_features = (
        cotangent.astype(jnp.float32) + conv(back_pre, kernel_one, True, rows, cols)
    ).astype(jnp.bfloat16)
    return grad_features, grad_first, grad_second


def solution(mesh):
    in_specs = (
        P("lat", "lon", None),
        P("lat", "lon", None),
        P(("lat", "lon"), None),
        P(("lat", "lon"), None),
    )
    out_specs = (P("lat", "lon", None), P(("lat", "lon"), None), P(("lat", "lon"), None))
    return jax.shard_map(local, mesh=mesh, in_specs=in_specs, out_specs=out_specs, check_vma=False)
```

```python
import jax
import jax.numpy as jnp
from jax import lax
from jax.experimental import pallas as pl
from jax.experimental.pallas import tpu as pltpu
from jax.sharding import PartitionSpec as P

AXES = ("lat", "lon")
BF16 = jnp.bfloat16
F32 = jnp.float32


def ring(axis, step, periodic):
    count = lax.axis_size(axis)
    pairs = [(i, (i + step) % count) for i in range(count)]
    if not periodic:
        pairs = [(i, j) for i, j in pairs if j == i + step]
    return pairs


def exchange(fields):
    count, rows, cols, chans = fields.shape
    left = lax.ppermute(fields[:, :, -2:], "lon", ring("lon", 1, True))
    right = lax.ppermute(fields[:, :, :2], "lon", ring("lon", -1, True))
    gap = jnp.zeros((count, rows, 12, chans), fields.dtype)
    wide = jnp.concatenate([fields, right, gap, left], axis=2)
    above = lax.ppermute(wide[:, -2:], "lat", ring("lat", 1, False))
    below = lax.ppermute(wide[:, :2], "lat", ring("lat", -1, False))
    return wide, above, below


def gather_kernels(w_first, w_second):
    count = lax.axis_size(AXES)
    rows, chans = w_first.shape
    mine = jnp.stack([w_first, w_second], 1)[None]
    sent = jnp.broadcast_to(mine, (count, rows, 2, chans))
    got = lax.all_to_all(sent, AXES, 0, 0, tiled=True).reshape(-1, 2, chans)
    return got[:, 0], got[:, 1]


def scatter_sums(first, second):
    count = lax.axis_size(AXES)
    chans = first.shape[1]
    rows = first.shape[0] // count
    core = lax.axis_index(AXES) % 2
    both = jnp.stack([first, second], 1).reshape(count // 2, 2, rows, 2, chans)
    keep = lax.dynamic_index_in_dim(both, core, 1, keepdims=False)
    send = lax.dynamic_index_in_dim(both, 1 - core, 1, keepdims=False)
    got = lax.ppermute(send, AXES, [(i, i ^ 1) for i in range(count)])
    groups = [list(range(parity, count, 2)) for parity in range(2)]
    parts = lax.all_to_all(keep + got, AXES, 0, 0, tiled=True, axis_index_groups=groups)
    total = parts.sum(0)
    return total[:, 0], total[:, 1]


def prepare_kernel(wide_ref, above_ref, below_ref, taps_ref, cells_ref):
    pairs = taps_ref.shape[1]
    for field in range(2):
        for p in range(pairs):
            if p == 0:
                rows = [above_ref[field, r] for r in range(2)]
            elif p == pairs - 1:
                rows = [below_ref[field, r] for r in range(2)]
            else:
                rows = [wide_ref[field, 2 * p - 2 + r] for r in range(2)]
            centre = jnp.concatenate(rows, 1)
            wide = centre.astype(F32)
            size = wide.shape[0]
            taps = jnp.concatenate(
                [
                    pltpu.roll(wide, 1, 0).astype(BF16),
                    centre,
                    pltpu.roll(wide, size - 1, 0).astype(BF16),
                ],
                1,
            )
            taps_ref[field, p] = taps
            filled = jnp.concatenate([taps, jnp.zeros((256 - size, taps.shape[1]), BF16)], 0)
            cells_ref[field, :, 256 * p : 256 * (p + 1)] = filled.T


def prepare(wide, above, below):
    fields, rows, width, chans = wide.shape
    pairs = rows // 2 + 2
    whole = pl.BlockSpec(memory_space=pltpu.VMEM)
    return pl.pallas_call(
        prepare_kernel,
        out_shape=(
            jax.ShapeDtypeStruct((fields, pairs, width, 6 * chans), BF16),
            jax.ShapeDtypeStruct((fields, 6 * chans, 256 * pairs), BF16),
        ),
        in_specs=[whole] * 3,
        out_specs=(whole, whole),
    )(wide, above, below)


def tap_rows(a, b, chans):
    tap = (a + 1) * 3 + b + 1
    return slice(tap * chans, (tap + 1) * chans)


def fill_plain(weight_ref, table_ref):
    chans = weight_ref.shape[1]
    for half in range(2):
        for b in range(3):
            for source in range(2):
                for target in range(2):
                    a = 2 * half + source - target - 1
                    at = (2 * b + source) * chans
                    if abs(a) <= 1:
                        block = weight_ref[tap_rows(a, b - 1, chans)]
                    else:
                        block = jnp.zeros((chans, chans), BF16)
                    table_ref[half, at : at + chans, target * chans : (target + 1) * chans] = block


def fill_turned(weight_ref, table_ref):
    chans = weight_ref.shape[1]
    for half in range(2):
        for b in range(3):
            for source in range(2):
                for target in range(2):
                    a = 2 * half + source - target - 1
                    at = (2 * b + source) * chans
                    if abs(a) <= 1:
                        block = weight_ref[tap_rows(-a, 1 - b, chans)]
                    else:
                        block = jnp.zeros((chans, chans), BF16)
                    table_ref[half, target * chans : (target + 1) * chans, at : at + chans] = block


def plain(lhs, rhs):
    return lax.dot_general(lhs, rhs, (((1,), (0,)), ((), ())), preferred_element_type=F32)


def turned(lhs, rhs):
    return lax.dot_general(lhs, rhs, (((1,), (1,)), ((), ())), preferred_element_type=F32)


def middle_kernel(
    edge_ref, one_ref, two_ref, taps_ref, cells_ref,
    first_ref, second_ref, back_ref,
    plain_ref, turned_ref, act_ref, own_ref,
):
    pairs = back_ref.shape[0]
    width = back_ref.shape[1]
    chans = one_ref.shape[1]
    fill_plain(one_ref, plain_ref)
    fill_turned(two_ref, turned_ref)
    cols = width - 16
    act_ref[...] = jnp.zeros_like(act_ref)
    own_ref[...] = jnp.zeros_like(own_ref)
    lane = lax.broadcasted_iota(jnp.int32, (1, 2 * chans), 1)
    for p in range(pairs):
        pre = plain(taps_ref[0, p], plain_ref[0]) + plain(taps_ref[0, p + 1], plain_ref[1])
        back = turned(taps_ref[1, p], turned_ref[0]) + turned(taps_ref[1, p + 1], turned_ref[1])
        sigma = jax.nn.sigmoid(pre)
        act = pre * sigma
        back = back * sigma * (1.0 + pre * (1.0 - sigma))
        own = back
        if p == 0:
            rim = lane < chans
            back = jnp.where(rim & (edge_ref[0] == 1), 0.0, back)
        if p == pairs - 1:
            rim = lane >= chans
            back = jnp.where(rim & (edge_ref[1] == 1), 0.0, back)
        if p in (0, pairs - 1):
            act = jnp.where(rim, 0.0, act)
            own = jnp.where(rim, 0.0, own)
        back_ref[p] = back.astype(BF16)
        act_ref[256 * p : 256 * p + cols] = act[:cols].astype(BF16)
        own_ref[256 * p : 256 * p + cols] = own[:cols].astype(BF16)
    span = 256 * pairs
    firsts = [plain(cells_ref[0, :, 256 * d : 256 * d + span], own_ref[...]) for d in range(2)]
    seconds = [plain(cells_ref[1, :, 256 * d : 256 * d + span], act_ref[...]) for d in range(2)]
    for a in range(-1, 2):
        for b in range(3):

            def summed(halves):
                total = None
                for half in range(2):
                    for source in range(2):
                        target = 2 * half + source - 1 - a
                        if target in (0, 1):
                            at = (2 * b + source) * chans
                            block = halves[half][at : at + chans, target * chans : (target + 1) * chans]
                            total = block if total is None else total + block
                return total

            first_ref[tap_rows(a, b - 1, chans)] = summed(firsts)
            second_ref[tap_rows(-a, 1 - b, chans)] = summed(seconds).T


def middle(edges, one, two, taps, cells):
    _, pairs, width, lanes = taps.shape
    pairs -= 1
    chans = one.shape[1]
    whole = pl.BlockSpec(memory_space=pltpu.VMEM)
    sums = jax.ShapeDtypeStruct(one.shape, F32)
    return pl.pallas_call(
        middle_kernel,
        out_shape=(sums, sums, jax.ShapeDtypeStruct((pairs, width, 2 * chans), BF16)),
        in_specs=[pl.BlockSpec(memory_space=pltpu.SMEM)] + [whole] * 4,
        out_specs=(whole,) * 3,
        scratch_shapes=[
            pltpu.VMEM((2, lanes, 2 * chans), BF16),
            pltpu.VMEM((2, 2 * chans, lanes), BF16),
            pltpu.VMEM((256 * pairs, 2 * chans), BF16),
            pltpu.VMEM((256 * pairs, 2 * chans), BF16),
        ],
    )(edges, one, two, taps, cells)


def final_kernel(one_ref, back_ref, cot_ref, out_ref, turned_ref, taps_ref):
    fill_turned(one_ref, turned_ref)
    pairs, width, lanes = back_ref.shape
    rows, cols, chans = cot_ref.shape
    for p in range(pairs):
        centre = back_ref[p]
        wide = centre.astype(F32)
        taps_ref[p] = jnp.concatenate(
            [
                pltpu.roll(wide, 1, 0).astype(BF16),
                centre,
                pltpu.roll(wide, width - 1, 0).astype(BF16),
            ],
            1,
        )
    for p in range(rows // 2):
        total = turned(taps_ref[p, :cols], turned_ref[0]) + turned(
            taps_ref[p + 1, :cols], turned_ref[1]
        )
        for r in range(2):
            out_ref[2 * p + r] = (
                total[:, r * chans : (r + 1) * chans] + cot_ref[2 * p + r].astype(F32)
            ).astype(BF16)


def final(one, back, cotangent):
    pairs, width, lanes = back.shape
    whole = pl.BlockSpec(memory_space=pltpu.VMEM)
    return pl.pallas_call(
        final_kernel,
        out_shape=jax.ShapeDtypeStruct(cotangent.shape, BF16),
        in_specs=[whole] * 3,
        out_specs=whole,
        scratch_shapes=[
            pltpu.VMEM((2, lanes, 3 * lanes), BF16),
            pltpu.VMEM((pairs, width, 3 * lanes), BF16),
        ],
        cost_estimate=pl.CostEstimate(flops=2 * 1152 * 128 * 3072, bytes_accessed=4 << 20, transcendentals=0),
    )(one, back, cotangent)


def local(features, cotangent, w_first, w_second):
    one, two = gather_kernels(w_first, w_second)
    wide, above, below = exchange(jnp.stack([features, cotangent]))
    taps, cells = prepare(wide, above, below)
    place = lax.axis_index("lat")
    edges = jnp.stack([place == 0, place == lax.axis_size("lat") - 1]).astype(jnp.int32)
    first, second, back = middle(edges, one, two, taps, cells)
    grad_first, grad_second = scatter_sums(first, second)
    return final(one, back, cotangent), grad_first, grad_second


def solution(mesh):
    in_specs = (
        P("lat", "lon", None),
        P("lat", "lon", None),
        P(("lat", "lon"), None),
        P(("lat", "lon"), None),
    )
    out_specs = (P("lat", "lon", None), P(("lat", "lon"), None), P(("lat", "lon"), None))
    return jax.shard_map(local, mesh=mesh, in_specs=in_specs, out_specs=out_specs, check_vma=False)
```

```python
import jax
import jax.numpy as jnp
from jax import lax
from jax.experimental import pallas as pl
from jax.experimental.pallas import tpu as pltpu
from jax.sharding import PartitionSpec as P

AXES = ("lat", "lon")
BF16 = jnp.bfloat16
F32 = jnp.float32
PREP_LIMIT = 24 << 20
MIDDLE_LIMIT = 60 * 1024 * 1024
FINAL_LIMIT = 16 << 20


def ring(axis, step, periodic):
    count = lax.axis_size(axis)
    pairs = [(i, (i + step) % count) for i in range(count)]
    if not periodic:
        pairs = [(i, j) for i, j in pairs if j == i + step]
    return pairs


def gather_kernels(w_first, w_second):
    count = lax.axis_size(AXES)
    rows, chans = w_first.shape
    mine = jnp.stack([w_first, w_second], 1)[None]
    sent = jnp.broadcast_to(mine, (count, rows, 2, chans))
    return lax.all_to_all(sent, AXES, 0, 0, tiled=True).reshape(-1, chans)


def scatter_sums(sums):
    count = lax.axis_size(AXES)
    chans = sums.shape[1]
    rows = sums.shape[0] // (2 * count)
    core = lax.axis_index(AXES) % 2
    both = sums.reshape(count // 2, 2, rows, 2, chans)
    keep = lax.dynamic_index_in_dim(both, core, 1, keepdims=False)
    send = lax.dynamic_index_in_dim(both, 1 - core, 1, keepdims=False)
    got = lax.ppermute(send, AXES, [(i, i ^ 1) for i in range(count)])
    groups = [list(range(parity, count, 2)) for parity in range(2)]
    parts = lax.all_to_all(keep + got, AXES, 0, 0, tiled=True, axis_index_groups=groups)
    return add_parts(parts.reshape(-1, chans), count // 2, rows)


def add_kernel(parts_ref, first_ref, second_ref):
    rows = first_ref.shape[0]
    groups = parts_ref.shape[0] // (2 * rows)
    for r in range(rows):
        for out_ref, at in ((first_ref, 2 * r), (second_ref, 2 * r + 1)):
            out_ref[r : r + 1] = jnp.sum(
                parts_ref[pl.ds(at, groups, stride=2 * rows)], 0, keepdims=True
            )


def add_parts(parts, groups, rows):
    whole = pl.BlockSpec(memory_space=pltpu.VMEM)
    out = jax.ShapeDtypeStruct((rows, parts.shape[1]), F32)
    return pl.pallas_call(
        add_kernel, out_shape=(out, out), in_specs=[whole], out_specs=(whole, whole),
        compiler_params=pltpu.CompilerParams(vmem_limit_bytes=4 << 20),
    )(parts)


def column_taps(centre):
    wide = centre.astype(F32)
    return jnp.concatenate(
        [
            pltpu.roll(wide, 1, 0).astype(BF16),
            centre,
            pltpu.roll(wide, wide.shape[0] - 1, 0).astype(BF16),
        ],
        1,
    )


def inner_kernel(feat_ref, cot_ref, tail_ref, taps_ref, cells_ref):
    pairs = taps_ref.shape[1]
    cols = feat_ref.shape[1]
    for field, own_ref in enumerate((feat_ref, cot_ref)):
        last = None
        for p in range(pairs):
            rows = [
                jnp.concatenate([own_ref[r], tail_ref[field, r]], 0)
                for r in (2 * p + 1, 2 * p + 2)
            ]
            taps = column_taps(jnp.concatenate(rows, 1))
            taps_ref[field, p] = taps
            own = taps[:cols]
            if p:
                at = 2 * cols * ((p - 1) // 2)
                cells_ref[field, p % 2, :, at : at + 2 * cols] = jnp.concatenate([last, own], 0).T
            last = own


def inner(features, cotangent, tail):
    rows, cols, chans = features.shape
    width = cols + tail.shape[2]
    pairs = rows // 2 - 1
    whole = pl.BlockSpec(memory_space=pltpu.VMEM)
    return pl.pallas_call(
        inner_kernel,
        out_shape=(
            jax.ShapeDtypeStruct((2, pairs, width, 6 * chans), BF16),
            jax.ShapeDtypeStruct((2, 2, 6 * chans, cols * (pairs - 1)), BF16),
        ),
        in_specs=[whole] * 3,
        out_specs=(whole, whole),
        compiler_params=pltpu.CompilerParams(vmem_limit_bytes=PREP_LIMIT),
        cost_estimate=pl.CostEstimate(flops=1 << 32, bytes_accessed=16 << 20, transcendentals=0),
    )(features, cotangent, tail)


def outer_kernel(feat_ref, cot_ref, tail_ref, above_ref, below_ref, near_ref, taps_ref, cells_ref):
    rows, cols, _ = feat_ref.shape
    pairs = near_ref.shape[1]
    for field, own_ref in enumerate((feat_ref, cot_ref)):
        first = jnp.concatenate([own_ref[0], tail_ref[field, 0]], 0)
        taps = column_taps(jnp.concatenate([above_ref[field], first], 1))
        taps_ref[field, 0] = taps
        cells_ref[field, 0] = jnp.concatenate([taps[:cols], near_ref[field, 0, :cols]], 0).T
        last = jnp.concatenate([own_ref[rows - 1], tail_ref[field, rows - 1]], 0)
        taps = column_taps(jnp.concatenate([last, below_ref[field]], 1))
        taps_ref[field, 1] = taps
        cells_ref[field, 1] = jnp.concatenate([near_ref[field, pairs - 1, :cols], taps[:cols]], 0).T


def outer(features, cotangent, tail, above, below, near):
    rows, cols, chans = features.shape
    width = cols + tail.shape[2]
    whole = pl.BlockSpec(memory_space=pltpu.VMEM)
    return pl.pallas_call(
        outer_kernel,
        out_shape=(
            jax.ShapeDtypeStruct((2, 2, width, 6 * chans), BF16),
            jax.ShapeDtypeStruct((2, 2, 6 * chans, 2 * cols), BF16),
        ),
        in_specs=[whole] * 6,
        out_specs=(whole, whole),
        compiler_params=pltpu.CompilerParams(vmem_limit_bytes=PREP_LIMIT),
        cost_estimate=pl.CostEstimate(flops=1 << 30, bytes_accessed=4 << 20, transcendentals=0),
    )(features, cotangent, tail, above, below, near)


def tap_rows(a, b, chans):
    tap = (a + 1) * 3 + b + 1
    return slice(tap * chans, (tap + 1) * chans)


def fill_plain(weight_ref, table_ref):
    chans = weight_ref.shape[1]
    for half in range(2):
        for b in range(3):
            for source in range(2):
                for target in range(2):
                    a = 2 * half + source - target - 1
                    at = (2 * b + source) * chans
                    if abs(a) <= 1:
                        block = weight_ref[tap_rows(a, b - 1, chans)]
                    else:
                        block = jnp.zeros((chans, chans), BF16)
                    table_ref[half, at : at + chans, target * chans : (target + 1) * chans] = block


def fill_turned(weight_ref, table_ref):
    chans = weight_ref.shape[1]
    for half in range(2):
        for b in range(3):
            for source in range(2):
                for target in range(2):
                    a = 2 * half + source - target - 1
                    at = (2 * b + source) * chans
                    if abs(a) <= 1:
                        block = weight_ref[tap_rows(-a, 1 - b, chans)]
                    else:
                        block = jnp.zeros((chans, chans), BF16)
                    table_ref[half, target * chans : (target + 1) * chans, at : at + chans] = block


def plain(lhs, rhs):
    return lax.dot_general(lhs, rhs, (((1,), (0,)), ((), ())), preferred_element_type=F32)


def turned(lhs, rhs):
    return lax.dot_general(lhs, rhs, (((1,), (1,)), ((), ())), preferred_element_type=F32)


def middle_kernel(
    both_ref, inner_taps_ref, inner_cells_ref, outer_taps_ref, outer_cells_ref,
    sums_ref, back_ref,
    wide_ref, one_ref, two_ref, plain_ref, turned_ref, slope_ref, act_ref, own_ref,
    taps_ref, cells_ref, taps_sem, cells_sem,
):
    pairs, width, lanes = back_ref.shape
    inner_cols = inner_cells_ref.shape[3]
    outer_cols = outer_cells_ref.shape[3]
    loads = {}
    for c in range(2):
        for field in range(2):
            loads[c, field] = (
                pltpu.make_async_copy(
                    outer_taps_ref.at[field, c],
                    taps_ref.at[field, pairs * c],
                    taps_sem.at[c, field, 0],
                ),
                pltpu.make_async_copy(
                    inner_taps_ref.at[field, pl.ds(c * pairs // 2, pairs // 2 - c)],
                    taps_ref.at[field, pl.ds(c * pairs // 2 + 1, pairs // 2 - c)],
                    taps_sem.at[c, field, 1],
                ),
            )
            for load in loads[c, field]:
                load.start()
    cell_loads = {}
    for field in (1, 0):
        for shift in range(2):
            cell_loads[field, shift] = (
                pltpu.make_async_copy(
                    outer_cells_ref.at[field, shift],
                    cells_ref.at[field, shift, :, pl.ds(shift * inner_cols, outer_cols)],
                    cells_sem.at[field, shift, 0],
                ),
                pltpu.make_async_copy(
                    inner_cells_ref.at[field, shift],
                    cells_ref.at[field, shift, :, pl.ds((1 - shift) * outer_cols, inner_cols)],
                    cells_sem.at[field, shift, 1],
                ),
            )
            for load in cell_loads[field, shift]:
                load.start()
    chans = lanes // 2
    cols = width - 16
    taps = one_ref.shape[0]
    wide_ref[...] = both_ref[...].astype(F32)
    one_ref[...] = wide_ref[pl.ds(0, taps, stride=2)].astype(BF16)
    two_ref[...] = wide_ref[pl.ds(1, taps, stride=2)].astype(BF16)
    fill_plain(one_ref, plain_ref)
    fill_turned(two_ref, turned_ref)

    def rows_of(field, first, count):
        return taps_ref[field, first : first + count].reshape(count * width, 3 * lanes)

    def cells_of(field, shift):
        for load in cell_loads[field, shift]:
            load.wait()
        return cells_ref[field, shift]

    step = pairs // 2
    for c in range(0, pairs, step):
        for load in loads[c // step, 0]:
            load.wait()
        pre = plain(rows_of(0, c, step), plain_ref[0]) + plain(rows_of(0, c + 1, step), plain_ref[1])
        sigma = jax.nn.sigmoid(pre)
        act = (pre * sigma).astype(BF16)
        slope_ref[...] = sigma * (1.0 + pre * (1.0 - sigma))
        for p in range(step):
            at = cols * (c + p)
            act_ref[at : at + cols] = act[width * p : width * p + cols]
        for load in loads[c // step, 1]:
            load.wait()
        back = turned(rows_of(1, c, step), turned_ref[0]) + turned(
            rows_of(1, c + 1, step), turned_ref[1]
        )
        back = (back * slope_ref[...]).astype(BF16)
        for p in range(step):
            at = cols * (c + p)
            part = back[width * p : width * (p + 1)]
            back_ref[c + p] = part
            own_ref[at : at + cols] = part[:cols]
    seconds = [plain(cells_of(1, d), act_ref[...]) for d in range(2)]
    firsts = [plain(cells_of(0, d), own_ref[...]) for d in range(2)]
    for a in range(-1, 2):
        for b in range(3):

            def summed(halves):
                total = None
                for half in range(2):
                    for source in range(2):
                        target = 2 * half + source - 1 - a
                        if target in (0, 1):
                            at = (2 * b + source) * chans
                            block = halves[half][at : at + chans, target * chans : (target + 1) * chans]
                            total = block if total is None else total + block
                return total

            at = tap_rows(a, b - 1, chans).start
            sums_ref[pl.ds(2 * at, chans, stride=2)] = summed(firsts)
            at = tap_rows(-a, 1 - b, chans).start
            sums_ref[pl.ds(2 * at + 1, chans, stride=2)] = summed(seconds).T


def middle(both, inner_parts, outer_parts):
    inner_taps, inner_cells = inner_parts
    outer_taps, outer_cells = outer_parts
    pairs = inner_taps.shape[1] + 1
    width = inner_taps.shape[2]
    rows, chans = both.shape
    lanes = 2 * chans
    cells = pairs * (width - 16)
    whole = pl.BlockSpec(memory_space=pltpu.VMEM)
    return pl.pallas_call(
        middle_kernel,
        out_shape=(
            jax.ShapeDtypeStruct((rows, chans), F32),
            jax.ShapeDtypeStruct((pairs, width, lanes), BF16),
        ),
        in_specs=[whole] + [pl.BlockSpec(memory_space=pltpu.HBM)] * 4,
        out_specs=(whole,) * 2,
        scratch_shapes=[
            pltpu.VMEM((rows, chans), F32),
            pltpu.VMEM((rows // 2, chans), BF16),
            pltpu.VMEM((rows // 2, chans), BF16),
            pltpu.VMEM((2, 3 * lanes, lanes), BF16),
            pltpu.VMEM((2, lanes, 3 * lanes), BF16),
            pltpu.VMEM((pairs // 2 * width, lanes), F32),
            pltpu.VMEM((cells, lanes), BF16),
            pltpu.VMEM((cells, lanes), BF16),
            pltpu.VMEM((2, pairs + 1, width, 3 * lanes), BF16),
            pltpu.VMEM((2, 2, 3 * lanes, cells), BF16),
            pltpu.SemaphoreType.DMA((2, 2, 2)),
            pltpu.SemaphoreType.DMA((2, 2, 2)),
        ],
        compiler_params=pltpu.CompilerParams(vmem_limit_bytes=MIDDLE_LIMIT),
    )(both, inner_taps, inner_cells, outer_taps, outer_cells)


def final_kernel(
    both_ref, back_ref, above_ref, below_ref, cot_ref, out_ref,
    wide_ref, one_ref, turned_ref, taps_ref,
):
    pairs, width, lanes = back_ref.shape
    rows, cols, chans = cot_ref.shape
    wide_ref[...] = both_ref[...].astype(F32)
    one_ref[...] = wide_ref[pl.ds(0, one_ref.shape[0], stride=2)].astype(BF16)
    fill_turned(one_ref, turned_ref)
    for p in range(pairs + 1):
        low = above_ref[...] if p == 0 else back_ref[p - 1, :, chans:]
        high = below_ref[...] if p == pairs else back_ref[p, :, :chans]
        taps = column_taps(jnp.concatenate([low, high], 1))
        taps_ref[cols * p : cols * (p + 1)] = taps[:cols]
    step = pairs // 2
    for c in range(0, pairs, step):
        total = turned(taps_ref[cols * c : cols * (c + step)], turned_ref[0]) + turned(
            taps_ref[cols * (c + 1) : cols * (c + step + 1)], turned_ref[1]
        )
        for p in range(step):
            for r in range(2):
                row = 2 * (c + p) + r
                part = total[cols * p : cols * (p + 1), r * chans : (r + 1) * chans]
                out_ref[row] = (part + cot_ref[row].astype(F32)).astype(BF16)


def final(both, back, above, below, cotangent):
    pairs, width, lanes = back.shape
    rows, cols, chans = cotangent.shape
    whole = pl.BlockSpec(memory_space=pltpu.VMEM)
    return pl.pallas_call(
        final_kernel,
        out_shape=jax.ShapeDtypeStruct(cotangent.shape, BF16),
        in_specs=[whole] * 5,
        out_specs=whole,
        scratch_shapes=[
            pltpu.VMEM(both.shape, F32),
            pltpu.VMEM((both.shape[0] // 2, chans), BF16),
            pltpu.VMEM((2, lanes, 3 * lanes), BF16),
            pltpu.VMEM(((pairs + 1) * cols, 3 * lanes), BF16),
        ],
        compiler_params=pltpu.CompilerParams(vmem_limit_bytes=FINAL_LIMIT),
        cost_estimate=pl.CostEstimate(flops=1 << 32, bytes_accessed=8 << 20, transcendentals=0),
    )(both, back, above, below, cotangent)


def shift_rows(top, bottom):
    above = lax.ppermute(bottom, "lat", ring("lat", 1, False))
    below = lax.ppermute(top, "lat", ring("lat", -1, False))
    return above, below


def local(features, cotangent, w_first, w_second):
    both = gather_kernels(w_first, w_second)
    rows, cols, chans = features.shape
    left = jnp.stack([features[:, -2:], cotangent[:, -2:]])
    right = jnp.stack([features[:, :2], cotangent[:, :2]])
    left = lax.ppermute(left, "lon", ring("lon", 1, True))
    right = lax.ppermute(right, "lon", ring("lon", -1, True))
    tail = jnp.concatenate([right, jnp.zeros((2, rows, 12, chans), BF16), left], 2)

    def whole_row(r):
        return jnp.concatenate([jnp.stack([features[r], cotangent[r]]), tail[:, r]], 1)

    above, below = shift_rows(whole_row(0), whole_row(rows - 1))
    inner_parts = inner(features, cotangent, tail)
    outer_parts = outer(features, cotangent, tail, above, below, inner_parts[0])
    sums, back = middle(both, inner_parts, outer_parts)
    grads = scatter_sums(sums)
    above, below = shift_rows(back[0, :, :chans], back[-1, :, chans:])
    return final(both, back, above, below, cotangent), *grads


def solution(mesh):
    in_specs = (
        P("lat", "lon", None),
        P("lat", "lon", None),
        P(("lat", "lon"), None),
        P(("lat", "lon"), None),
    )
    out_specs = (P("lat", "lon", None), P(("lat", "lon"), None), P(("lat", "lon"), None))
    return jax.shard_map(local, mesh=mesh, in_specs=in_specs, out_specs=out_specs, check_vma=False)
```

```python
import functools

import jax
import jax.numpy as jnp
from jax import lax
from jax.experimental import pallas as pl
from jax.experimental.pallas import tpu as pltpu
from jax.sharding import PartitionSpec as P


AXES = ("lat", "lon")
BF16 = jnp.bfloat16
F32 = jnp.float32
PREP_LIMIT = 4 << 20
MIDDLE_LIMIT = 12 << 20
FINAL_LIMIT = 12 << 20


def ring(axis, step, periodic):
    count = lax.axis_size(axis)
    pairs = [(i, (i + step) % count) for i in range(count)]
    if not periodic:
        pairs = [(i, j) for i, j in pairs if j == i + step]
    return pairs


def gather_kernels(w_first, w_second):
    count = lax.axis_size(AXES)
    rows, chans = w_first.shape
    mine = jnp.stack([w_first, w_second], 1)[None]
    sent = jnp.broadcast_to(mine, (count, rows, 2, chans))
    return lax.all_to_all(sent, AXES, 0, 0, tiled=True).reshape(-1, chans)


def scatter_sums(keep, send):
    count = lax.axis_size(AXES)
    rows, chans = keep.shape
    rows //= count
    got = lax.ppermute(send, AXES, [(i, i ^ 1) for i in range(count)])
    groups = [list(range(parity, count, 2)) for parity in range(2)]
    parts = join(keep, got).reshape(count // 2, rows, 2, chans)
    parts = lax.all_to_all(parts, AXES, 0, 0, tiled=True, axis_index_groups=groups)
    return add_parts(parts.reshape(-1, chans), rows)


def join_kernel(keep_ref, got_ref, out_ref):
    out_ref[...] = keep_ref[...] + got_ref[...]


def join(keep, got):
    whole = pl.BlockSpec(memory_space=pltpu.VMEM)
    return pl.pallas_call(
        join_kernel, out_shape=jax.ShapeDtypeStruct(keep.shape, F32),
        in_specs=[whole] * 2, out_specs=whole,
        compiler_params=pltpu.CompilerParams(vmem_limit_bytes=4 << 20),
    )(keep, got)


def add_kernel(parts_ref, first_ref, second_ref):
    rows = first_ref.shape[0]
    groups = parts_ref.shape[0] // (2 * rows)
    for r in range(rows):
        for out_ref, at in ((first_ref, 2 * r), (second_ref, 2 * r + 1)):
            out_ref[r : r + 1] = jnp.sum(
                parts_ref[pl.ds(at, groups, stride=2 * rows)], 0, keepdims=True
            )


def add_parts(parts, rows):
    whole = pl.BlockSpec(memory_space=pltpu.VMEM)
    out = jax.ShapeDtypeStruct((rows, parts.shape[1]), F32)
    return pl.pallas_call(
        add_kernel, out_shape=(out, out), in_specs=[whole], out_specs=(whole, whole),
        compiler_params=pltpu.CompilerParams(vmem_limit_bytes=4 << 20),
    )(parts)


def shifted(row):
    wide = row.astype(F32)
    left = pltpu.roll(wide, 1, 0).astype(BF16)
    right = pltpu.roll(wide, wide.shape[0] - 1, 0).astype(BF16)
    return left, row, right


def paired(first, second):
    return jnp.concatenate([part for both in zip(first, second) for part in both], 1)


def inner_kernel(feat_ref, cot_ref, tail_ref, taps_ref, cells_ref):
    rows, cols, _ = feat_ref.shape
    for field, own_ref in enumerate((feat_ref, cot_ref)):
        seen = [
            shifted(jnp.concatenate([own_ref[r], tail_ref[field, r]], 0)) for r in range(rows)
        ]
        for p in range(rows // 2):
            taps_ref[field, p] = paired(seen[2 * p], seen[2 * p + 1])
        pairs = [paired(seen[r], seen[r + 1])[:cols] for r in range(1, rows - 2, 2)]
        for p in range(len(pairs) - 1):
            at = 2 * cols * (p // 2)
            cells_ref[field, 1 - p % 2, :, at : at + 2 * cols] = jnp.concatenate(
                pairs[p : p + 2], 0
            ).T


def inner(features, cotangent, tail):
    rows, cols, chans = features.shape
    width = cols + tail.shape[2]
    whole = pl.BlockSpec(memory_space=pltpu.VMEM)
    return pl.pallas_call(
        inner_kernel,
        out_shape=(
            jax.ShapeDtypeStruct((2, rows // 2, width, 6 * chans), BF16),
            jax.ShapeDtypeStruct((2, 2, 6 * chans, cols * (rows // 2 - 2)), BF16),
        ),
        in_specs=[whole] * 3,
        out_specs=(whole, whole),
        compiler_params=pltpu.CompilerParams(vmem_limit_bytes=PREP_LIMIT),
        cost_estimate=pl.CostEstimate(flops=1 << 32, bytes_accessed=16 << 20, transcendentals=0),
    )(features, cotangent, tail)


def outer_kernel(above_ref, below_ref, near_ref, taps_ref, cells_ref):
    pairs = near_ref.shape[1]
    chans = above_ref.shape[3]
    cols = cells_ref.shape[3] // 2
    for field in range(2):

        def near(r):
            p, r = divmod(r % (2 * pairs), 2)
            at = [(2 * b + r) * chans for b in range(3)]
            return [near_ref[field, p, :, i : i + chans] for i in at]

        above = [shifted(above_ref[field, r]) for r in range(2)]
        below = [shifted(below_ref[field, r]) for r in range(2)]
        taps_ref[field, 0] = paired(*above)
        taps_ref[field, 1] = paired(*below)
        cells = [paired(above[1], near(0)), paired(near(1), near(2))]
        cells_ref[field, 0] = jnp.concatenate([cell[:cols] for cell in cells], 0).T
        cells = [paired(near(-3), near(-2)), paired(near(-1), below[0])]
        cells_ref[field, 1] = jnp.concatenate([cell[:cols] for cell in cells], 0).T


def outer(above, below, near, cols):
    _, _, width, chans = above.shape
    whole = pl.BlockSpec(memory_space=pltpu.VMEM)
    return pl.pallas_call(
        outer_kernel,
        out_shape=(
            jax.ShapeDtypeStruct((2, 2, width, 6 * chans), BF16),
            jax.ShapeDtypeStruct((2, 2, 6 * chans, 2 * cols), BF16),
        ),
        in_specs=[whole] * 3,
        out_specs=(whole, whole),
        compiler_params=pltpu.CompilerParams(vmem_limit_bytes=PREP_LIMIT),
        cost_estimate=pl.CostEstimate(flops=1 << 30, bytes_accessed=4 << 20, transcendentals=0),
    )(above, below, near)


def tap_rows(a, b, chans):
    tap = (a + 1) * 3 + b + 1
    return slice(tap * chans, (tap + 1) * chans)


def fill_plain(weight_ref, table_ref):
    chans = weight_ref.shape[1]
    for half in range(2):
        for b in range(3):
            for source in range(2):
                for target in range(2):
                    a = 2 * half + source - target - 1
                    at = (2 * b + source) * chans
                    if abs(a) <= 1:
                        block = weight_ref[tap_rows(a, b - 1, chans)]
                    else:
                        block = jnp.zeros((chans, chans), BF16)
                    table_ref[half, at : at + chans, target * chans : (target + 1) * chans] = block


def fill_turned(weight_ref, table_ref):
    chans = weight_ref.shape[1]
    for half in range(2):
        for b in range(3):
            for source in range(2):
                for target in range(2):
                    a = 2 * half + source - target - 1
                    at = (2 * b + source) * chans
                    if abs(a) <= 1:
                        block = weight_ref[tap_rows(-a, 1 - b, chans)]
                    else:
                        block = jnp.zeros((chans, chans), BF16)
                    table_ref[half, target * chans : (target + 1) * chans, at : at + chans] = block


def plain(lhs, rhs):
    return lax.dot_general(lhs, rhs, (((1,), (0,)), ((), ())), preferred_element_type=F32)


def turned(lhs, rhs):
    return lax.dot_general(lhs, rhs, (((1,), (1,)), ((), ())), preferred_element_type=F32)


def middle_kernel(
    own_rows, place_ref, both_ref, inner_taps_ref, inner_cells_ref, outer_taps_ref, outer_cells_ref,
    keep_ref, send_ref, back_ref,
    wide_ref, sums_ref, one_ref, two_ref, plain_ref, turned_ref, slope_ref, act_ref, own_ref,
):
    pairs, width, lanes = back_ref.shape
    chans = lanes // 2
    cols = width - 16
    taps = one_ref.shape[0]
    wide_ref[...] = both_ref[...].astype(F32)
    one_ref[...] = wide_ref[pl.ds(0, taps, stride=2)].astype(BF16)
    two_ref[...] = wide_ref[pl.ds(1, taps, stride=2)].astype(BF16)
    fill_plain(one_ref, plain_ref)
    fill_turned(two_ref, turned_ref)

    def rows_of(field, first, count):
        parts = []
        for p in range(first, first + count):
            if p == 0:
                parts.append(outer_taps_ref[field, 0])
            elif p == pairs:
                parts.append(outer_taps_ref[field, 1])
            else:
                parts.append(inner_taps_ref[field, p - 1])
        return jnp.concatenate(parts, 0)

    def cells_of(field, shift):
        parts = [outer_cells_ref[field, shift], inner_cells_ref[field, shift]]
        return jnp.concatenate(parts if shift == 0 else parts[::-1], 1)

    lane = lax.broadcasted_iota(jnp.int32, (1, lanes), 1)
    step = pairs // 3
    for c in range(0, pairs, step):
        pre = plain(rows_of(0, c, step), plain_ref[0]) + plain(rows_of(0, c + 1, step), plain_ref[1])
        sigma = jax.nn.sigmoid(pre)
        act = (pre * sigma).astype(BF16)
        slope_ref[...] = sigma * (1.0 + pre * (1.0 - sigma))
        back = turned(rows_of(1, c, step), turned_ref[0]) + turned(
            rows_of(1, c + 1, step), turned_ref[1]
        )
        back = (back * slope_ref[...]).astype(BF16)
        for p in range(step):
            part = back[width * p : width * (p + 1)]
            for out_ref, rows in ((act_ref, act[width * p : width * p + cols]), (own_ref, part[:cols])):
                at = cols * (c + p)
                if c + p < pairs - 1:
                    out_ref[at : at + cols, :chans] = rows[:, chans:]
                if c + p > 0:
                    out_ref[at - cols : at, chans:] = rows[:, :chans]
            if c + p == 0:
                part = jnp.where((lane < chans) & (place_ref[1] == 1), 0.0, part.astype(F32)).astype(BF16)
            if c + p == pairs - 1:
                part = jnp.where((lane >= chans) & (place_ref[2] == 1), 0.0, part.astype(F32)).astype(BF16)
            back_ref[c + p] = part
    seconds = [plain(cells_of(1, d), act_ref[...]) for d in range(2)]
    firsts = [plain(cells_of(0, d), own_ref[...]) for d in range(2)]
    for a in range(-1, 2):
        for b in range(3):

            def summed(halves):
                total = None
                for half in range(2):
                    for source in range(2):
                        target = 2 * half + source - 1 - a
                        if target in (0, 1):
                            at = (2 * b + source) * chans
                            block = halves[half][at : at + chans, target * chans : (target + 1) * chans]
                            total = block if total is None else total + block
                return total

            at = tap_rows(a, b - 1, chans).start
            sums_ref[pl.ds(2 * at, chans, stride=2)] = summed(firsts)
            at = tap_rows(-a, 1 - b, chans).start
            sums_ref[pl.ds(2 * at + 1, chans, stride=2)] = summed(seconds).T
    core = place_ref[0]
    groups = keep_ref.shape[0] // own_rows
    for g in range(groups):
        out = pl.ds(own_rows * g, own_rows)
        keep_ref[out] = sums_ref[pl.ds(own_rows * (2 * g + core), own_rows)]
        send_ref[out] = sums_ref[pl.ds(own_rows * (2 * g + 1 - core), own_rows)]


def middle(place, both, inner_parts, outer_parts, own_rows):
    inner_taps, inner_cells = inner_parts
    outer_taps, outer_cells = outer_parts
    pairs = inner_taps.shape[1] + 1
    width = inner_taps.shape[2]
    rows, chans = both.shape
    lanes = 2 * chans
    cells = (pairs - 1) * (width - 16)
    whole = pl.BlockSpec(memory_space=pltpu.VMEM)
    return pl.pallas_call(
        functools.partial(middle_kernel, own_rows),
        out_shape=(
            jax.ShapeDtypeStruct((rows // 2, chans), F32),
            jax.ShapeDtypeStruct((rows // 2, chans), F32),
            jax.ShapeDtypeStruct((pairs, width, lanes), BF16),
        ),
        in_specs=[pl.BlockSpec(memory_space=pltpu.SMEM)] + [whole] * 5,
        out_specs=(whole,) * 3,
        scratch_shapes=[
            pltpu.VMEM((rows, chans), F32),
            pltpu.VMEM((rows, chans), F32),
            pltpu.VMEM((rows // 2, chans), BF16),
            pltpu.VMEM((rows // 2, chans), BF16),
            pltpu.VMEM((2, 3 * lanes, lanes), BF16),
            pltpu.VMEM((2, lanes, 3 * lanes), BF16),
            pltpu.VMEM((pairs // 3 * width, lanes), F32),
            pltpu.VMEM((cells, lanes), BF16),
            pltpu.VMEM((cells, lanes), BF16),
        ],
        compiler_params=pltpu.CompilerParams(vmem_limit_bytes=MIDDLE_LIMIT),
    )(place, both, inner_taps, inner_cells, outer_taps, outer_cells)


def final_kernel(both_ref, back_ref, cot_ref, out_ref, wide_ref, one_ref, turned_ref, taps_ref):
    pairs, _, _ = back_ref.shape
    _, cols, chans = cot_ref.shape
    wide_ref[...] = both_ref[...].astype(F32)
    one_ref[...] = wide_ref[pl.ds(0, one_ref.shape[0], stride=2)].astype(BF16)
    fill_turned(one_ref, turned_ref)
    for p in range(pairs):
        taps = jnp.concatenate(shifted(back_ref[p]), 1)
        taps_ref[cols * p : cols * (p + 1)] = taps[:cols]
    step = (pairs - 1) // 2
    for c in range(0, pairs - 1, step):
        total = turned(taps_ref[cols * c : cols * (c + step)], turned_ref[0]) + turned(
            taps_ref[cols * (c + 1) : cols * (c + step + 1)], turned_ref[1]
        )
        for p in range(step):
            for r in range(2):
                row = 2 * (c + p) + r
                part = total[cols * p : cols * (p + 1), r * chans : (r + 1) * chans]
                out_ref[row] = (part + cot_ref[row].astype(F32)).astype(BF16)


def final(both, back, cotangent):
    pairs, _, lanes = back.shape
    _, cols, chans = cotangent.shape
    whole = pl.BlockSpec(memory_space=pltpu.VMEM)
    return pl.pallas_call(
        final_kernel,
        out_shape=jax.ShapeDtypeStruct(cotangent.shape, BF16),
        in_specs=[whole] * 3,
        out_specs=whole,
        scratch_shapes=[
            pltpu.VMEM(both.shape, F32),
            pltpu.VMEM((both.shape[0] // 2, chans), BF16),
            pltpu.VMEM((2, lanes, 3 * lanes), BF16),
            pltpu.VMEM((pairs * cols, 3 * lanes), BF16),
        ],
        compiler_params=pltpu.CompilerParams(vmem_limit_bytes=FINAL_LIMIT),
        cost_estimate=pl.CostEstimate(flops=1 << 32, bytes_accessed=8 << 20, transcendentals=0),
    )(both, back, cotangent)


def layer(features, cotangent, w_first, w_second):
    both = gather_kernels(w_first, w_second)
    rows, cols, chans = features.shape
    left = jnp.stack([features[:, -2:], cotangent[:, -2:]])
    right = jnp.stack([features[:, :2], cotangent[:, :2]])
    left = lax.ppermute(left, "lon", ring("lon", 1, True))
    right = lax.ppermute(right, "lon", ring("lon", -1, True))
    tail = jnp.concatenate([right, jnp.zeros((2, rows, 12, chans), BF16), left], 2)

    def whole_rows(at):
        return jnp.concatenate([jnp.stack([features[at], cotangent[at]]), tail[:, at]], 2)

    above = lax.ppermute(whole_rows(slice(rows - 2, rows)), "lat", ring("lat", 1, False))
    below = lax.ppermute(whole_rows(slice(0, 2)), "lat", ring("lat", -1, False))
    at = lax.axis_index("lat")
    place = jnp.stack(
        [
            lax.axis_index(AXES) % 2,
            (at == 0).astype(jnp.int32),
            (at == lax.axis_size("lat") - 1).astype(jnp.int32),
        ]
    )
    both, own_tail = lax.optimization_barrier((both, tail))
    inner_parts = inner(features, cotangent, own_tail)
    outer_parts = outer(above, below, inner_parts[0], cols)
    keep, send, back = middle(place, both, inner_parts, outer_parts, 2 * w_first.shape[0])
    grads = scatter_sums(keep, send)
    return final(both, back, cotangent), *grads


def solution(mesh):
    in_specs = (
        P("lat", "lon", None),
        P("lat", "lon", None),
        P(("lat", "lon"), None),
        P(("lat", "lon"), None),
    )
    out_specs = (P("lat", "lon", None), P(("lat", "lon"), None), P(("lat", "lon"), None))
    return jax.shard_map(layer, mesh=mesh, in_specs=in_specs, out_specs=out_specs, check_vma=False)
```

```python
import functools

import jax
import jax.numpy as jnp
from jax import lax
from jax.experimental import pallas as pl
from jax.experimental.pallas import tpu as pltpu
from jax.sharding import PartitionSpec as P


AXES = ("lat", "lon")
BF16 = jnp.bfloat16
F32 = jnp.float32
PREP_LIMIT = 4 << 20
MIDDLE_LIMIT = 12 << 20
FINAL_LIMIT = 12 << 20


def swap(sent, axis, odd_first, periodic):
    count = lax.axis_size(axis)
    pairs = [(i, (i + 1) % count) for i in range(odd_first, count, 2)]
    if not periodic:
        pairs = [(i, j) for i, j in pairs if j == i + 1]
    return lax.ppermute(sent, axis, pairs + [(j, i) for i, j in pairs])


def spread_kernel(first_ref, second_ref, out_ref, mixed_ref):
    rows, _ = first_ref.shape
    first, second = first_ref[...].astype(F32), second_ref[...].astype(F32)
    blocks = mixed_ref.shape[0] // (2 * rows)
    for block in range(blocks):
        at = 2 * rows * block
        mixed_ref[pl.ds(at, rows, stride=2)] = first
        mixed_ref[pl.ds(at + 1, rows, stride=2)] = second
    mixed = mixed_ref[...].astype(BF16)
    for at in range(0, out_ref.shape[0], mixed.shape[0]):
        out_ref[at : at + mixed.shape[0]] = mixed


def spread(w_first, w_second, count):
    rows, chans = w_first.shape
    whole = pl.BlockSpec(memory_space=pltpu.VMEM)
    return pl.pallas_call(
        spread_kernel,
        out_shape=jax.ShapeDtypeStruct((2 * rows * count, chans), BF16),
        in_specs=[whole] * 2,
        out_specs=whole,
        scratch_shapes=[pltpu.VMEM((2 * rows * min(8, count), chans), F32)],
        compiler_params=pltpu.CompilerParams(vmem_limit_bytes=4 << 20),
    )(w_first, w_second)


def gather_kernels(w_first, w_second):
    count = lax.axis_size(AXES)
    rows, chans = w_first.shape
    sent = spread(w_first, w_second, count // 2).reshape(count // 2, rows, 2, chans)
    groups = [list(range(parity, count, 2)) for parity in range(2)]
    mine = lax.all_to_all(sent, AXES, 0, 0, tiled=True, axis_index_groups=groups)
    mine = mine.reshape(-1, chans)
    return mine, lax.ppermute(mine, AXES, [(i, i ^ 1) for i in range(count)])


def scatter_sums(keep, send):
    count = lax.axis_size(AXES)
    rows, chans = keep.shape
    rows //= count
    got = lax.ppermute(send, AXES, [(i, i ^ 1) for i in range(count)])
    groups = [list(range(parity, count, 2)) for parity in range(2)]
    parts = join(keep, got).reshape(count // 2, rows, 2, chans)
    parts = lax.all_to_all(parts, AXES, 0, 0, tiled=True, axis_index_groups=groups)
    return add_parts(parts.reshape(-1, chans), rows)


def join_kernel(keep_ref, got_ref, out_ref):
    out_ref[...] = keep_ref[...] + got_ref[...]


def join(keep, got):
    whole = pl.BlockSpec(memory_space=pltpu.VMEM)
    return pl.pallas_call(
        join_kernel, out_shape=jax.ShapeDtypeStruct(keep.shape, F32),
        in_specs=[whole] * 2, out_specs=whole,
        compiler_params=pltpu.CompilerParams(vmem_limit_bytes=4 << 20),
    )(keep, got)


def add_kernel(parts_ref, first_ref, second_ref):
    rows = first_ref.shape[0]
    groups = parts_ref.shape[0] // (2 * rows)
    for r in range(rows):
        for out_ref, at in ((first_ref, 2 * r), (second_ref, 2 * r + 1)):
            out_ref[r : r + 1] = jnp.sum(
                parts_ref[pl.ds(at, groups, stride=2 * rows)], 0, keepdims=True
            )


def add_parts(parts, rows):
    whole = pl.BlockSpec(memory_space=pltpu.VMEM)
    out = jax.ShapeDtypeStruct((rows, parts.shape[1]), F32)
    return pl.pallas_call(
        add_kernel, out_shape=(out, out), in_specs=[whole], out_specs=(whole, whole),
        compiler_params=pltpu.CompilerParams(vmem_limit_bytes=4 << 20),
    )(parts)


def shifted(row):
    wide = row.astype(F32)
    left = pltpu.roll(wide, 1, 0).astype(BF16)
    right = pltpu.roll(wide, wide.shape[0] - 1, 0).astype(BF16)
    return left, row, right


def paired(first, second):
    return jnp.concatenate([part for both in zip(first, second) for part in both], 1)


def inner_kernel(feat_ref, cot_ref, tail_ref, taps_ref, cells_ref):
    rows, cols, _ = feat_ref.shape
    for field, own_ref in enumerate((feat_ref, cot_ref)):
        seen = [
            shifted(jnp.concatenate([own_ref[r], tail_ref[field, r]], 0)) for r in range(rows)
        ]
        for p in range(rows // 2):
            taps_ref[field, p] = paired(seen[2 * p], seen[2 * p + 1])
        pairs = [paired(seen[r], seen[r + 1])[:cols] for r in range(1, rows - 2, 2)]
        for p in range(len(pairs) - 1):
            at = 2 * cols * (p // 2)
            cells_ref[field, 1 - p % 2, :, at : at + 2 * cols] = jnp.concatenate(
                pairs[p : p + 2], 0
            ).T


def inner(features, cotangent, tail):
    rows, cols, chans = features.shape
    width = cols + tail.shape[2]
    whole = pl.BlockSpec(memory_space=pltpu.VMEM)
    return pl.pallas_call(
        inner_kernel,
        out_shape=(
            jax.ShapeDtypeStruct((2, rows // 2, width, 6 * chans), BF16),
            jax.ShapeDtypeStruct((2, 2, 6 * chans, cols * (rows // 2 - 2)), BF16),
        ),
        in_specs=[whole] * 3,
        out_specs=(whole, whole),
        compiler_params=pltpu.CompilerParams(vmem_limit_bytes=PREP_LIMIT),
        cost_estimate=pl.CostEstimate(flops=1 << 32, bytes_accessed=16 << 20, transcendentals=0),
    )(features, cotangent, tail)


def outer_kernel(
    place_ref, even_ref, odd_ref, near_ref, taps_ref, cells_ref
):
    pairs = near_ref.shape[1]
    chans = even_ref.shape[3]
    cols = cells_ref.shape[3] // 2
    odd = place_ref[3] == 1

    def whole(first_ref, second_ref, at):
        return jnp.where(odd, first_ref[at].astype(F32), second_ref[at].astype(F32)).astype(BF16)

    for field in range(2):

        def near(r):
            p, r = divmod(r % (2 * pairs), 2)
            at = [(2 * b + r) * chans for b in range(3)]
            return [near_ref[field, p, :, i : i + chans] for i in at]

        above = [shifted(whole(even_ref, odd_ref, (field, r))) for r in range(2)]
        below = [shifted(whole(odd_ref, even_ref, (field, r))) for r in range(2)]
        taps_ref[field, 0] = paired(*above)
        taps_ref[field, 1] = paired(*below)
        cells = [paired(above[1], near(0)), paired(near(1), near(2))]
        cells_ref[field, 0] = jnp.concatenate([cell[:cols] for cell in cells], 0).T
        cells = [paired(near(-3), near(-2)), paired(near(-1), below[0])]
        cells_ref[field, 1] = jnp.concatenate([cell[:cols] for cell in cells], 0).T


def outer(place, rims, near, cols):
    _, _, width, chans = rims[0].shape
    whole = pl.BlockSpec(memory_space=pltpu.VMEM)
    return pl.pallas_call(
        outer_kernel,
        out_shape=(
            jax.ShapeDtypeStruct((2, 2, width, 6 * chans), BF16),
            jax.ShapeDtypeStruct((2, 2, 6 * chans, 2 * cols), BF16),
        ),
        in_specs=[pl.BlockSpec(memory_space=pltpu.SMEM)] + [whole] * 3,
        out_specs=(whole, whole),
        compiler_params=pltpu.CompilerParams(vmem_limit_bytes=PREP_LIMIT),
        cost_estimate=pl.CostEstimate(flops=1 << 30, bytes_accessed=4 << 20, transcendentals=0),
    )(place, *rims, near)


def tap_rows(a, b, chans):
    tap = (a + 1) * 3 + b + 1
    return slice(tap * chans, (tap + 1) * chans)


def fill_plain(weight_ref, table_ref):
    chans = weight_ref.shape[1]
    for half in range(2):
        for b in range(3):
            for source in range(2):
                for target in range(2):
                    a = 2 * half + source - target - 1
                    at = (2 * b + source) * chans
                    if abs(a) <= 1:
                        block = weight_ref[tap_rows(a, b - 1, chans)]
                    else:
                        block = jnp.zeros((chans, chans), BF16)
                    table_ref[half, at : at + chans, target * chans : (target + 1) * chans] = block


def fill_turned(weight_ref, table_ref):
    chans = weight_ref.shape[1]
    for half in range(2):
        for b in range(3):
            for source in range(2):
                for target in range(2):
                    a = 2 * half + source - target - 1
                    at = (2 * b + source) * chans
                    if abs(a) <= 1:
                        block = weight_ref[tap_rows(-a, 1 - b, chans)]
                    else:
                        block = jnp.zeros((chans, chans), BF16)
                    table_ref[half, target * chans : (target + 1) * chans, at : at + chans] = block


def plain(lhs, rhs):
    return lax.dot_general(lhs, rhs, (((1,), (0,)), ((), ())), preferred_element_type=F32)


def turned(lhs, rhs):
    return lax.dot_general(lhs, rhs, (((1,), (1,)), ((), ())), preferred_element_type=F32)


def middle_kernel(
    own_rows, place_ref, mine_ref, other_ref, inner_taps_ref, inner_cells_ref, outer_taps_ref, outer_cells_ref,
    keep_ref, send_ref, back_ref, one_ref,
    mixed_ref, wide_ref, sums_ref, two_ref, plain_ref, turned_ref, slope_ref, act_ref, own_ref,
):
    pairs, width, lanes = back_ref.shape
    chans = lanes // 2
    cols = width - 16
    taps = one_ref.shape[0]
    core = place_ref[0]
    mixed_ref[0] = mine_ref[...].astype(F32)
    mixed_ref[1] = other_ref[...].astype(F32)
    for g in range(mine_ref.shape[0] // own_rows):
        at = own_rows * g
        mine, other = (mixed_ref[i, at : at + own_rows] for i in range(2))
        wide_ref[2 * at : 2 * at + own_rows] = jnp.where(core == 0, mine, other)
        wide_ref[2 * at + own_rows : 2 * at + 2 * own_rows] = jnp.where(core == 0, other, mine)
    one_ref[...] = wide_ref[pl.ds(0, taps, stride=2)].astype(BF16)
    two_ref[...] = wide_ref[pl.ds(1, taps, stride=2)].astype(BF16)
    fill_plain(one_ref, plain_ref)
    fill_turned(two_ref, turned_ref)

    def rows_of(field, first, count):
        parts = []
        for p in range(first, first + count):
            if p == 0:
                parts.append(outer_taps_ref[field, 0])
            elif p == pairs:
                parts.append(outer_taps_ref[field, 1])
            else:
                parts.append(inner_taps_ref[field, p - 1])
        return jnp.concatenate(parts, 0)

    def cells_of(field, shift):
        parts = [outer_cells_ref[field, shift], inner_cells_ref[field, shift]]
        return jnp.concatenate(parts if shift == 0 else parts[::-1], 1)

    lane = lax.broadcasted_iota(jnp.int32, (1, lanes), 1)
    step = pairs // 3
    for c in range(0, pairs, step):
        pre = plain(rows_of(0, c, step), plain_ref[0]) + plain(rows_of(0, c + 1, step), plain_ref[1])
        sigma = jax.nn.sigmoid(pre)
        act = (pre * sigma).astype(BF16)
        slope_ref[...] = sigma * (1.0 + pre * (1.0 - sigma))
        back = turned(rows_of(1, c, step), turned_ref[0]) + turned(
            rows_of(1, c + 1, step), turned_ref[1]
        )
        back = (back * slope_ref[...]).astype(BF16)
        for p in range(step):
            part = back[width * p : width * (p + 1)]
            for out_ref, rows in ((act_ref, act[width * p : width * p + cols]), (own_ref, part[:cols])):
                at = cols * (c + p)
                if c + p < pairs - 1:
                    out_ref[at : at + cols, :chans] = rows[:, chans:]
                if c + p > 0:
                    out_ref[at - cols : at, chans:] = rows[:, :chans]
            if c + p == 0:
                part = jnp.where((lane < chans) & (place_ref[1] == 1), 0.0, part.astype(F32)).astype(BF16)
            if c + p == pairs - 1:
                part = jnp.where((lane >= chans) & (place_ref[2] == 1), 0.0, part.astype(F32)).astype(BF16)
            back_ref[c + p] = part
    seconds = [plain(cells_of(1, d), act_ref[...]) for d in range(2)]
    firsts = [plain(cells_of(0, d), own_ref[...]) for d in range(2)]
    for a in range(-1, 2):
        for b in range(3):

            def summed(halves):
                total = None
                for half in range(2):
                    for source in range(2):
                        target = 2 * half + source - 1 - a
                        if target in (0, 1):
                            at = (2 * b + source) * chans
                            block = halves[half][at : at + chans, target * chans : (target + 1) * chans]
                            total = block if total is None else total + block
                return total

            at = tap_rows(a, b - 1, chans).start
            sums_ref[pl.ds(2 * at, chans, stride=2)] = summed(firsts)
            at = tap_rows(-a, 1 - b, chans).start
            sums_ref[pl.ds(2 * at + 1, chans, stride=2)] = summed(seconds).T
    groups = keep_ref.shape[0] // own_rows
    for g in range(groups):
        out = pl.ds(own_rows * g, own_rows)
        keep_ref[out] = sums_ref[pl.ds(own_rows * (2 * g + core), own_rows)]
        send_ref[out] = sums_ref[pl.ds(own_rows * (2 * g + 1 - core), own_rows)]


def middle(place, both, inner_parts, outer_parts, own_rows):
    inner_taps, inner_cells = inner_parts
    outer_taps, outer_cells = outer_parts
    pairs = inner_taps.shape[1] + 1
    width = inner_taps.shape[2]
    rows, chans = both[0].shape
    rows *= 2
    lanes = 2 * chans
    cells = (pairs - 1) * (width - 16)
    whole = pl.BlockSpec(memory_space=pltpu.VMEM)
    return pl.pallas_call(
        functools.partial(middle_kernel, own_rows),
        out_shape=(
            jax.ShapeDtypeStruct((rows // 2, chans), F32),
            jax.ShapeDtypeStruct((rows // 2, chans), F32),
            jax.ShapeDtypeStruct((pairs, width, lanes), BF16),
            jax.ShapeDtypeStruct((rows // 2, chans), BF16),
        ),
        in_specs=[pl.BlockSpec(memory_space=pltpu.SMEM)] + [whole] * 6,
        out_specs=(whole,) * 4,
        scratch_shapes=[
            pltpu.VMEM((2, rows // 2, chans), F32),
            pltpu.VMEM((rows, chans), F32),
            pltpu.VMEM((rows, chans), F32),
            pltpu.VMEM((rows // 2, chans), BF16),
            pltpu.VMEM((2, 3 * lanes, lanes), BF16),
            pltpu.VMEM((2, lanes, 3 * lanes), BF16),
            pltpu.VMEM((pairs // 3 * width, lanes), F32),
            pltpu.VMEM((cells, lanes), BF16),
            pltpu.VMEM((cells, lanes), BF16),
        ],
        compiler_params=pltpu.CompilerParams(vmem_limit_bytes=MIDDLE_LIMIT),
    )(place, *both, inner_taps, inner_cells, outer_taps, outer_cells)


def final_kernel(one_ref, back_ref, cot_ref, out_ref, turned_ref, taps_ref):
    pairs, _, _ = back_ref.shape
    _, cols, chans = cot_ref.shape
    fill_turned(one_ref, turned_ref)
    for p in range(pairs):
        taps = jnp.concatenate(shifted(back_ref[p]), 1)
        taps_ref[cols * p : cols * (p + 1)] = taps[:cols]
    step = (pairs - 1) // 2
    for c in range(0, pairs - 1, step):
        total = turned(taps_ref[cols * c : cols * (c + step)], turned_ref[0]) + turned(
            taps_ref[cols * (c + 1) : cols * (c + step + 1)], turned_ref[1]
        )
        for p in range(step):
            for r in range(2):
                row = 2 * (c + p) + r
                part = total[cols * p : cols * (p + 1), r * chans : (r + 1) * chans]
                out_ref[row] = (part + cot_ref[row].astype(F32)).astype(BF16)


def final(one, back, cotangent):
    pairs, _, lanes = back.shape
    _, cols, _ = cotangent.shape
    whole = pl.BlockSpec(memory_space=pltpu.VMEM)
    return pl.pallas_call(
        final_kernel,
        out_shape=jax.ShapeDtypeStruct(cotangent.shape, BF16),
        in_specs=[whole] * 3,
        out_specs=whole,
        scratch_shapes=[
            pltpu.VMEM((2, lanes, 3 * lanes), BF16),
            pltpu.VMEM((pairs * cols, 3 * lanes), BF16),
        ],
        compiler_params=pltpu.CompilerParams(vmem_limit_bytes=FINAL_LIMIT),
        cost_estimate=pl.CostEstimate(flops=1 << 32, bytes_accessed=8 << 20, transcendentals=0),
    )(one, back, cotangent)


def layer(features, cotangent, w_first, w_second):
    both = gather_kernels(w_first, w_second)
    rows, cols, chans = features.shape
    lon, lat = lax.axis_index("lon"), lax.axis_index("lat")

    def edge(field, axis, first):
        size = field.shape[axis]
        start = jnp.where(first, 0, size - 2)
        return lax.dynamic_slice_in_dim(field, start, 2, axis)

    def edges(axis, first):
        return jnp.stack([edge(features, axis, first), edge(cotangent, axis, first)])

    lat_odd, lon_odd = lat % 2 == 1, lon % 2 == 1
    rims, sides = [None, None], [None, None]
    for turn in (1, 0):
        sides[turn] = swap(edges(1, lon_odd ^ (turn == 1)), "lon", turn, True)
    right = jnp.where(lon_odd, sides[1], sides[0])
    left = jnp.where(lon_odd, sides[0], sides[1])
    tail = jnp.concatenate([right, jnp.zeros((2, rows, 12, chans), BF16), left], 2)
    for turn in (1, 0):
        first = lat_odd ^ (turn == 1)
        sent = jnp.concatenate([edges(0, first), edge(tail, 1, first)], 2)
        rims[turn] = swap(sent, "lat", turn, False)
    place = jnp.stack(
        [
            (lax.axis_index(AXES) % 2).astype(jnp.int32),
            (lat == 0).astype(jnp.int32),
            (lat == lax.axis_size("lat") - 1).astype(jnp.int32),
            lat_odd.astype(jnp.int32),
        ]
    )
    _, own_tail = lax.optimization_barrier((both[0], tail))
    inner_parts = inner(features, cotangent, own_tail)
    outer_parts = outer(place, rims, inner_parts[0], cols)
    keep, send, back, one = middle(place, both, inner_parts, outer_parts, 2 * w_first.shape[0])
    grads = scatter_sums(keep, send)
    return final(one, back, cotangent), *grads


def solution(mesh):
    in_specs = (
        P("lat", "lon", None),
        P("lat", "lon", None),
        P(("lat", "lon"), None),
        P(("lat", "lon"), None),
    )
    out_specs = (P("lat", "lon", None), P(("lat", "lon"), None), P(("lat", "lon"), None))
    return jax.shard_map(layer, mesh=mesh, in_specs=in_specs, out_specs=out_specs, check_vma=False)
```

```python
import functools

import jax
import jax.numpy as jnp
from jax import lax
from jax.experimental import pallas as pl
from jax.experimental.pallas import tpu as pltpu
from jax.sharding import PartitionSpec as P


AXES = ("lat", "lon")
BF16 = jnp.bfloat16
F32 = jnp.float32
SPREAD_LIMIT = 60 * 1024 * 1024
PREP_LIMIT = 4 << 20
MIDDLE_LIMIT = 12 << 20
FINAL_LIMIT = 12 << 20


def swap(sent, axis, odd_first, periodic):
    count = lax.axis_size(axis)
    pairs = [(i, (i + 1) % count) for i in range(odd_first, count, 2)]
    if not periodic:
        pairs = [(i, j) for i, j in pairs if j == i + 1]
    return lax.ppermute(sent, axis, pairs + [(j, i) for i, j in pairs])


def spread_kernel(first_ref, second_ref, out_ref, kernel_ref, mixed_ref, sems):
    rows, _ = first_ref.shape
    loads = [
        pltpu.make_async_copy(source, kernel_ref.at[i], sems.at[i])
        for i, source in enumerate((first_ref, second_ref))
    ]
    for load in loads:
        load.start()
    for load in loads:
        load.wait()
    first, second = kernel_ref[0].astype(F32), kernel_ref[1].astype(F32)
    blocks = mixed_ref.shape[0] // (2 * rows)
    for block in range(blocks):
        at = 2 * rows * block
        mixed_ref[pl.ds(at, rows, stride=2)] = first
        mixed_ref[pl.ds(at + 1, rows, stride=2)] = second
    mixed = mixed_ref[...].astype(BF16)
    for at in range(0, out_ref.shape[0], mixed.shape[0]):
        out_ref[at : at + mixed.shape[0]] = mixed


def spread(w_first, w_second, count):
    rows, chans = w_first.shape
    whole = pl.BlockSpec(memory_space=pltpu.VMEM)
    return pl.pallas_call(
        spread_kernel,
        out_shape=jax.ShapeDtypeStruct((2 * rows * count, chans), BF16),
        in_specs=[pl.BlockSpec(memory_space=pl.ANY)] * 2,
        out_specs=whole,
        scratch_shapes=[
            pltpu.VMEM((2, rows, chans), BF16),
            pltpu.VMEM((2 * rows * min(8, count), chans), F32),
            pltpu.SemaphoreType.DMA((2,)),
        ],
        compiler_params=pltpu.CompilerParams(vmem_limit_bytes=SPREAD_LIMIT),
    )(w_first, w_second)


def gather_kernels(w_first, w_second):
    count = lax.axis_size(AXES)
    rows, chans = w_first.shape
    sent = spread(w_first, w_second, count // 2).reshape(count // 2, rows, 2, chans)
    groups = [list(range(parity, count, 2)) for parity in range(2)]
    mine = lax.all_to_all(sent, AXES, 0, 0, tiled=True, axis_index_groups=groups)
    mine = mine.reshape(-1, chans)
    return mine, lax.ppermute(mine, AXES, [(i, i ^ 1) for i in range(count)])


def scatter_sums(keep, send):
    count = lax.axis_size(AXES)
    rows, chans = keep.shape
    rows //= count
    got = lax.ppermute(send, AXES, [(i, i ^ 1) for i in range(count)])
    groups = [list(range(parity, count, 2)) for parity in range(2)]
    parts = join(keep, got).reshape(count // 2, rows, 2, chans)
    parts = lax.all_to_all(parts, AXES, 0, 0, tiled=True, axis_index_groups=groups)
    return add_parts(parts.reshape(-1, chans), rows)


def join_kernel(keep_ref, got_ref, out_ref):
    out_ref[...] = keep_ref[...] + got_ref[...]


def join(keep, got):
    whole = pl.BlockSpec(memory_space=pltpu.VMEM)
    return pl.pallas_call(
        join_kernel, out_shape=jax.ShapeDtypeStruct(keep.shape, F32),
        in_specs=[whole] * 2, out_specs=whole,
        compiler_params=pltpu.CompilerParams(vmem_limit_bytes=4 << 20),
    )(keep, got)


def add_kernel(parts_ref, first_ref, second_ref):
    rows = first_ref.shape[0]
    groups = parts_ref.shape[0] // (2 * rows)
    for r in range(rows):
        for out_ref, at in ((first_ref, 2 * r), (second_ref, 2 * r + 1)):
            out_ref[r : r + 1] = jnp.sum(
                parts_ref[pl.ds(at, groups, stride=2 * rows)], 0, keepdims=True
            )


def add_parts(parts, rows):
    whole = pl.BlockSpec(memory_space=pltpu.VMEM)
    out = jax.ShapeDtypeStruct((rows, parts.shape[1]), F32)
    return pl.pallas_call(
        add_kernel, out_shape=(out, out), in_specs=[whole], out_specs=(whole, whole),
        compiler_params=pltpu.CompilerParams(vmem_limit_bytes=4 << 20),
    )(parts)


def shifted(row):
    wide = row.astype(F32)
    left = pltpu.roll(wide, 1, 0).astype(BF16)
    right = pltpu.roll(wide, wide.shape[0] - 1, 0).astype(BF16)
    return left, row, right


def paired(first, second):
    return jnp.concatenate([part for both in zip(first, second) for part in both], 1)


def stage_kernel(feat_ref, cot_ref, feat_out_ref, cot_out_ref):
    feat_out_ref[...] = feat_ref[...]
    cot_out_ref[...] = cot_ref[...]


def stage(features, cotangent):
    whole = pl.BlockSpec(memory_space=pltpu.VMEM)
    out = jax.ShapeDtypeStruct(features.shape, BF16)
    return pl.pallas_call(
        stage_kernel,
        out_shape=(out, out),
        in_specs=[whole] * 2,
        out_specs=(whole, whole),
        compiler_params=pltpu.CompilerParams(vmem_limit_bytes=PREP_LIMIT),
        cost_estimate=pl.CostEstimate(flops=1 << 30, bytes_accessed=4 << 20, transcendentals=0),
    )(features, cotangent)


def inner_kernel(feat_ref, cot_ref, tail_ref, taps_ref, cells_ref):
    rows, cols, _ = feat_ref.shape
    for field, own_ref in enumerate((feat_ref, cot_ref)):
        seen = [
            shifted(jnp.concatenate([own_ref[r], tail_ref[field, r]], 0)) for r in range(rows)
        ]
        for p in range(rows // 2):
            taps_ref[field, p] = paired(seen[2 * p], seen[2 * p + 1])
        pairs = [paired(seen[r], seen[r + 1])[:cols] for r in range(1, rows - 2, 2)]
        for p in range(len(pairs) - 1):
            at = 2 * cols * (p // 2)
            cells_ref[field, 1 - p % 2, :, at : at + 2 * cols] = jnp.concatenate(
                pairs[p : p + 2], 0
            ).T


def inner(features, cotangent, tail):
    rows, cols, chans = features.shape
    width = cols + tail.shape[2]
    whole = pl.BlockSpec(memory_space=pltpu.VMEM)
    return pl.pallas_call(
        inner_kernel,
        out_shape=(
            jax.ShapeDtypeStruct((2, rows // 2, width, 6 * chans), BF16),
            jax.ShapeDtypeStruct((2, 2, 6 * chans, cols * (rows // 2 - 2)), BF16),
        ),
        in_specs=[whole] * 3,
        out_specs=(whole, whole),
        compiler_params=pltpu.CompilerParams(vmem_limit_bytes=PREP_LIMIT),
        cost_estimate=pl.CostEstimate(flops=1 << 32, bytes_accessed=16 << 20, transcendentals=0),
    )(features, cotangent, tail)


def outer_kernel(
    even_ref, odd_ref, near_ref, taps_ref, cells_ref
):
    pairs = near_ref.shape[1]
    chans = even_ref.shape[3]
    cols = cells_ref.shape[3] // 2
    odd = lax.axis_index("lat") % 2 == 1

    def whole(first_ref, second_ref, at):
        return jnp.where(odd, first_ref[at].astype(F32), second_ref[at].astype(F32)).astype(BF16)

    for field in range(2):

        def near(r):
            p, r = divmod(r % (2 * pairs), 2)
            at = [(2 * b + r) * chans for b in range(3)]
            return [near_ref[field, p, :, i : i + chans] for i in at]

        above = [shifted(whole(even_ref, odd_ref, (field, r))) for r in range(2)]
        below = [shifted(whole(odd_ref, even_ref, (field, r))) for r in range(2)]
        taps_ref[field, 0] = paired(*above)
        taps_ref[field, 1] = paired(*below)
        cells = [paired(above[1], near(0)), paired(near(1), near(2))]
        cells_ref[field, 0] = jnp.concatenate([cell[:cols] for cell in cells], 0).T
        cells = [paired(near(-3), near(-2)), paired(near(-1), below[0])]
        cells_ref[field, 1] = jnp.concatenate([cell[:cols] for cell in cells], 0).T


def outer(rims, near, cols):
    _, _, width, chans = rims[0].shape
    whole = pl.BlockSpec(memory_space=pltpu.VMEM)
    return pl.pallas_call(
        outer_kernel,
        out_shape=(
            jax.ShapeDtypeStruct((2, 2, width, 6 * chans), BF16),
            jax.ShapeDtypeStruct((2, 2, 6 * chans, 2 * cols), BF16),
        ),
        in_specs=[whole] * 3,
        out_specs=(whole, whole),
        compiler_params=pltpu.CompilerParams(vmem_limit_bytes=PREP_LIMIT),
        cost_estimate=pl.CostEstimate(flops=1 << 30, bytes_accessed=4 << 20, transcendentals=0),
    )(*rims, near)


def tap_rows(a, b, chans):
    tap = (a + 1) * 3 + b + 1
    return slice(tap * chans, (tap + 1) * chans)


def fill_plain(weight_ref, table_ref):
    chans = weight_ref.shape[1]
    for half in range(2):
        for b in range(3):
            for source in range(2):
                for target in range(2):
                    a = 2 * half + source - target - 1
                    at = (2 * b + source) * chans
                    if abs(a) <= 1:
                        block = weight_ref[tap_rows(a, b - 1, chans)]
                    else:
                        block = jnp.zeros((chans, chans), BF16)
                    table_ref[half, at : at + chans, target * chans : (target + 1) * chans] = block


def fill_turned(weight_ref, table_ref):
    chans = weight_ref.shape[1]
    for half in range(2):
        for b in range(3):
            for source in range(2):
                for target in range(2):
                    a = 2 * half + source - target - 1
                    at = (2 * b + source) * chans
                    if abs(a) <= 1:
                        block = weight_ref[tap_rows(-a, 1 - b, chans)]
                    else:
                        block = jnp.zeros((chans, chans), BF16)
                    table_ref[half, target * chans : (target + 1) * chans, at : at + chans] = block


def plain(lhs, rhs):
    return lax.dot_general(lhs, rhs, (((1,), (0,)), ((), ())), preferred_element_type=F32)


def turned(lhs, rhs):
    return lax.dot_general(lhs, rhs, (((1,), (1,)), ((), ())), preferred_element_type=F32)


def middle_kernel(
    own_rows, mine_ref, other_ref, inner_taps_ref, inner_cells_ref, outer_taps_ref, outer_cells_ref,
    keep_ref, send_ref, back_ref, one_ref,
    mixed_ref, wide_ref, sums_ref, two_ref, plain_ref, turned_ref, slope_ref, act_ref, own_ref,
):
    pairs, width, lanes = back_ref.shape
    chans = lanes // 2
    cols = width - 16
    taps = one_ref.shape[0]
    core = lax.axis_index(AXES) % 2
    lat = lax.axis_index("lat")
    mixed_ref[0] = mine_ref[...].astype(F32)
    mixed_ref[1] = other_ref[...].astype(F32)
    for g in range(mine_ref.shape[0] // own_rows):
        at = own_rows * g
        mine, other = (mixed_ref[i, at : at + own_rows] for i in range(2))
        wide_ref[2 * at : 2 * at + own_rows] = jnp.where(core == 0, mine, other)
        wide_ref[2 * at + own_rows : 2 * at + 2 * own_rows] = jnp.where(core == 0, other, mine)
    one_ref[...] = wide_ref[pl.ds(0, taps, stride=2)].astype(BF16)
    two_ref[...] = wide_ref[pl.ds(1, taps, stride=2)].astype(BF16)
    fill_plain(one_ref, plain_ref)
    fill_turned(two_ref, turned_ref)

    def rows_of(field, first, count):
        parts = []
        for p in range(first, first + count):
            if p == 0:
                parts.append(outer_taps_ref[field, 0])
            elif p == pairs:
                parts.append(outer_taps_ref[field, 1])
            else:
                parts.append(inner_taps_ref[field, p - 1])
        return jnp.concatenate(parts, 0)

    def cells_of(field, shift):
        parts = [outer_cells_ref[field, shift], inner_cells_ref[field, shift]]
        return jnp.concatenate(parts if shift == 0 else parts[::-1], 1)

    lane = lax.broadcasted_iota(jnp.int32, (1, lanes), 1)
    step = pairs // 3
    for c in range(0, pairs, step):
        pre = plain(rows_of(0, c, step), plain_ref[0]) + plain(rows_of(0, c + 1, step), plain_ref[1])
        sigma = jax.nn.sigmoid(pre)
        act = (pre * sigma).astype(BF16)
        slope_ref[...] = sigma * (1.0 + pre * (1.0 - sigma))
        back = turned(rows_of(1, c, step), turned_ref[0]) + turned(
            rows_of(1, c + 1, step), turned_ref[1]
        )
        back = (back * slope_ref[...]).astype(BF16)
        for p in range(step):
            part = back[width * p : width * (p + 1)]
            for out_ref, rows in ((act_ref, act[width * p : width * p + cols]), (own_ref, part[:cols])):
                at = cols * (c + p)
                if c + p < pairs - 1:
                    out_ref[at : at + cols, :chans] = rows[:, chans:]
                if c + p > 0:
                    out_ref[at - cols : at, chans:] = rows[:, :chans]
            if c + p == 0:
                part = jnp.where((lane < chans) & (lat == 0), 0.0, part.astype(F32)).astype(BF16)
            if c + p == pairs - 1:
                part = jnp.where((lane >= chans) & (lat == lax.axis_size("lat") - 1), 0.0, part.astype(F32)).astype(BF16)
            back_ref[c + p] = part
    seconds = [plain(cells_of(1, d), act_ref[...]) for d in range(2)]
    firsts = [plain(cells_of(0, d), own_ref[...]) for d in range(2)]
    for a in range(-1, 2):
        for b in range(3):

            def summed(halves):
                total = None
                for half in range(2):
                    for source in range(2):
                        target = 2 * half + source - 1 - a
                        if target in (0, 1):
                            at = (2 * b + source) * chans
                            block = halves[half][at : at + chans, target * chans : (target + 1) * chans]
                            total = block if total is None else total + block
                return total

            at = tap_rows(a, b - 1, chans).start
            sums_ref[pl.ds(2 * at, chans, stride=2)] = summed(firsts)
            at = tap_rows(-a, 1 - b, chans).start
            sums_ref[pl.ds(2 * at + 1, chans, stride=2)] = summed(seconds).T
    groups = keep_ref.shape[0] // own_rows
    for g in range(groups):
        out = pl.ds(own_rows * g, own_rows)
        keep_ref[out] = sums_ref[pl.ds(own_rows * (2 * g + core), own_rows)]
        send_ref[out] = sums_ref[pl.ds(own_rows * (2 * g + 1 - core), own_rows)]


def middle(both, inner_parts, outer_parts, own_rows):
    inner_taps, inner_cells = inner_parts
    outer_taps, outer_cells = outer_parts
    pairs = inner_taps.shape[1] + 1
    width = inner_taps.shape[2]
    rows, chans = both[0].shape
    rows *= 2
    lanes = 2 * chans
    cells = (pairs - 1) * (width - 16)
    whole = pl.BlockSpec(memory_space=pltpu.VMEM)
    return pl.pallas_call(
        functools.partial(middle_kernel, own_rows),
        out_shape=(
            jax.ShapeDtypeStruct((rows // 2, chans), F32),
            jax.ShapeDtypeStruct((rows // 2, chans), F32),
            jax.ShapeDtypeStruct((pairs, width, lanes), BF16),
            jax.ShapeDtypeStruct((rows // 2, chans), BF16),
        ),
        in_specs=[whole] * 6,
        out_specs=(whole,) * 4,
        scratch_shapes=[
            pltpu.VMEM((2, rows // 2, chans), F32),
            pltpu.VMEM((rows, chans), F32),
            pltpu.VMEM((rows, chans), F32),
            pltpu.VMEM((rows // 2, chans), BF16),
            pltpu.VMEM((2, 3 * lanes, lanes), BF16),
            pltpu.VMEM((2, lanes, 3 * lanes), BF16),
            pltpu.VMEM((pairs // 3 * width, lanes), F32),
            pltpu.VMEM((cells, lanes), BF16),
            pltpu.VMEM((cells, lanes), BF16),
        ],
        compiler_params=pltpu.CompilerParams(vmem_limit_bytes=MIDDLE_LIMIT),
    )(*both, inner_taps, inner_cells, outer_taps, outer_cells)


def final_kernel(one_ref, back_ref, cot_ref, out_ref, turned_ref, taps_ref):
    pairs, _, _ = back_ref.shape
    _, cols, chans = cot_ref.shape
    fill_turned(one_ref, turned_ref)
    for p in range(pairs):
        taps = jnp.concatenate(shifted(back_ref[p]), 1)
        taps_ref[cols * p : cols * (p + 1)] = taps[:cols]
    step = (pairs - 1) // 2
    for c in range(0, pairs - 1, step):
        total = turned(taps_ref[cols * c : cols * (c + step)], turned_ref[0]) + turned(
            taps_ref[cols * (c + 1) : cols * (c + step + 1)], turned_ref[1]
        )
        for p in range(step):
            for r in range(2):
                row = 2 * (c + p) + r
                part = total[cols * p : cols * (p + 1), r * chans : (r + 1) * chans]
                out_ref[row] = (part + cot_ref[row].astype(F32)).astype(BF16)


def final(one, back, cotangent):
    pairs, _, lanes = back.shape
    _, cols, _ = cotangent.shape
    whole = pl.BlockSpec(memory_space=pltpu.VMEM)
    return pl.pallas_call(
        final_kernel,
        out_shape=jax.ShapeDtypeStruct(cotangent.shape, BF16),
        in_specs=[whole] * 3,
        out_specs=whole,
        scratch_shapes=[
            pltpu.VMEM((2, lanes, 3 * lanes), BF16),
            pltpu.VMEM((pairs * cols, 3 * lanes), BF16),
        ],
        compiler_params=pltpu.CompilerParams(vmem_limit_bytes=FINAL_LIMIT),
        cost_estimate=pl.CostEstimate(flops=1 << 32, bytes_accessed=8 << 20, transcendentals=0),
    )(one, back, cotangent)


def layer(features, cotangent, w_first, w_second):
    both = gather_kernels(w_first, w_second)
    rows, cols, chans = features.shape
    lon, lat = lax.axis_index("lon"), lax.axis_index("lat")

    def edge(field, axis, first):
        size = field.shape[axis]
        start = jnp.where(first, 0, size - 2)
        return lax.dynamic_slice_in_dim(field, start, 2, axis)

    def edges(axis, first):
        return jnp.stack([edge(features, axis, first), edge(cotangent, axis, first)])

    lat_odd, lon_odd = lat % 2 == 1, lon % 2 == 1
    rims, sides = [None, None], [None, None]
    for turn in (1, 0):
        sides[turn] = swap(edges(1, lon_odd ^ (turn == 1)), "lon", turn, True)
    right = jnp.where(lon_odd, sides[1], sides[0])
    left = jnp.where(lon_odd, sides[0], sides[1])
    tail = jnp.concatenate([right, jnp.zeros((2, rows, 12, chans), BF16), left], 2)
    for turn in (1, 0):
        first = lat_odd ^ (turn == 1)
        sent = jnp.concatenate([edges(0, first), edge(tail, 1, first)], 2)
        rims[turn] = swap(sent, "lat", turn, False)
    staged = stage(features, cotangent)
    _, own_tail = lax.optimization_barrier((both[0], tail))
    inner_parts = inner(*staged, own_tail)
    outer_parts = outer(rims, inner_parts[0], cols)
    keep, send, back, one = middle(both, inner_parts, outer_parts, 2 * w_first.shape[0])
    grads = scatter_sums(keep, send)
    return final(one, back, cotangent), *grads


def solution(mesh):
    in_specs = (
        P("lat", "lon", None),
        P("lat", "lon", None),
        P(("lat", "lon"), None),
        P(("lat", "lon"), None),
    )
    out_specs = (P("lat", "lon", None), P(("lat", "lon"), None), P(("lat", "lon"), None))
    return jax.shard_map(layer, mesh=mesh, in_specs=in_specs, out_specs=out_specs, check_vma=False)
```

```python
import functools

import jax
import jax.numpy as jnp
from jax import lax
from jax.experimental import pallas as pl
from jax.experimental.pallas import tpu as pltpu
from jax.sharding import PartitionSpec as P


AXES = ("lat", "lon")
BF16 = jnp.bfloat16
F32 = jnp.float32
SPREAD_LIMIT = 60 * 1024 * 1024
PREP_LIMIT = 4 << 20
MIDDLE_LIMIT = 12 << 20
FINAL_LIMIT = 12 << 20


def swap(sent, axis, odd_first, periodic):
    count = lax.axis_size(axis)
    pairs = [(i, (i + 1) % count) for i in range(odd_first, count, 2)]
    if not periodic:
        pairs = [(i, j) for i, j in pairs if j == i + 1]
    return lax.ppermute(sent, axis, pairs + [(j, i) for i, j in pairs])


def spread_kernel(first_ref, second_ref, out_ref, kernel_ref, mixed_ref, sems):
    rows, _ = first_ref.shape
    loads = [
        pltpu.make_async_copy(source, kernel_ref.at[i], sems.at[i])
        for i, source in enumerate((first_ref, second_ref))
    ]
    for load in loads:
        load.start()
    for load in loads:
        load.wait()
    first, second = kernel_ref[0].astype(F32), kernel_ref[1].astype(F32)
    blocks = mixed_ref.shape[0] // (2 * rows)
    for block in range(blocks):
        at = 2 * rows * block
        mixed_ref[pl.ds(at, rows, stride=2)] = first
        mixed_ref[pl.ds(at + 1, rows, stride=2)] = second
    mixed = mixed_ref[...].astype(BF16)
    for at in range(0, out_ref.shape[0], mixed.shape[0]):
        out_ref[at : at + mixed.shape[0]] = mixed


def spread(w_first, w_second, count):
    rows, chans = w_first.shape
    whole = pl.BlockSpec(memory_space=pltpu.VMEM)
    return pl.pallas_call(
        spread_kernel,
        out_shape=jax.ShapeDtypeStruct((2 * rows * count, chans), BF16),
        in_specs=[pl.BlockSpec(memory_space=pl.ANY)] * 2,
        out_specs=whole,
        scratch_shapes=[
            pltpu.VMEM((2, rows, chans), BF16),
            pltpu.VMEM((2 * rows * min(8, count), chans), F32),
            pltpu.SemaphoreType.DMA((2,)),
        ],
        compiler_params=pltpu.CompilerParams(vmem_limit_bytes=SPREAD_LIMIT),
    )(w_first, w_second)


def gather_kernels(w_first, w_second):
    count = lax.axis_size(AXES)
    rows, chans = w_first.shape
    sent = spread(w_first, w_second, count // 2).reshape(count // 2, rows, 2, chans)
    groups = [list(range(parity, count, 2)) for parity in range(2)]
    mine = lax.all_to_all(sent, AXES, 0, 0, tiled=True, axis_index_groups=groups)
    mine = mine.reshape(-1, chans)
    return mine, lax.ppermute(mine, AXES, [(i, i ^ 1) for i in range(count)])


def scatter_sums(keep, send):
    count = lax.axis_size(AXES)
    rows, chans = keep.shape
    rows //= count
    got = lax.ppermute(send, AXES, [(i, i ^ 1) for i in range(count)])
    groups = [list(range(parity, count, 2)) for parity in range(2)]
    parts = join(keep, got).reshape(count // 2, rows, 2, chans)
    parts = lax.all_to_all(parts, AXES, 0, 0, tiled=True, axis_index_groups=groups)
    return add_parts(parts.reshape(-1, chans), rows)


def join_kernel(keep_ref, got_ref, out_ref):
    out_ref[...] = keep_ref[...] + got_ref[...]


def join(keep, got):
    whole = pl.BlockSpec(memory_space=pltpu.VMEM)
    return pl.pallas_call(
        join_kernel, out_shape=jax.ShapeDtypeStruct(keep.shape, F32),
        in_specs=[whole] * 2, out_specs=whole,
        compiler_params=pltpu.CompilerParams(vmem_limit_bytes=4 << 20),
    )(keep, got)


def add_kernel(parts_ref, first_ref, second_ref):
    rows = first_ref.shape[0]
    groups = parts_ref.shape[0] // (2 * rows)
    for r in range(rows):
        for out_ref, at in ((first_ref, 2 * r), (second_ref, 2 * r + 1)):
            out_ref[r : r + 1] = jnp.sum(
                parts_ref[pl.ds(at, groups, stride=2 * rows)], 0, keepdims=True
            )


def add_parts(parts, rows):
    whole = pl.BlockSpec(memory_space=pltpu.VMEM)
    out = jax.ShapeDtypeStruct((rows, parts.shape[1]), F32)
    return pl.pallas_call(
        add_kernel, out_shape=(out, out), in_specs=[whole], out_specs=(whole, whole),
        compiler_params=pltpu.CompilerParams(vmem_limit_bytes=4 << 20),
    )(parts)


def shifted(row):
    wide = row.astype(F32)
    left = pltpu.roll(wide, 1, 0).astype(BF16)
    right = pltpu.roll(wide, wide.shape[0] - 1, 0).astype(BF16)
    return left, row, right


def paired(first, second):
    return jnp.concatenate([part for both in zip(first, second) for part in both], 1)


def stage_kernel(own_ref, out_ref):
    out_ref[...] = own_ref[...]


def stage(own):
    whole = pl.BlockSpec(memory_space=pltpu.VMEM)
    return pl.pallas_call(
        stage_kernel,
        out_shape=jax.ShapeDtypeStruct(own.shape, BF16),
        in_specs=[whole],
        out_specs=whole,
        compiler_params=pltpu.CompilerParams(vmem_limit_bytes=PREP_LIMIT),
        cost_estimate=pl.CostEstimate(flops=1 << 30, bytes_accessed=2 << 20, transcendentals=0),
    )(own)


def inner_kernel(field, own_ref, tail_ref, taps_ref, cells_ref):
    rows, cols, _ = own_ref.shape
    seen = [shifted(jnp.concatenate([own_ref[r], tail_ref[field, r]], 0)) for r in range(rows)]
    for p in range(rows // 2):
        taps_ref[p] = paired(seen[2 * p], seen[2 * p + 1])
    pairs = [paired(seen[r], seen[r + 1])[:cols] for r in range(1, rows - 2, 2)]
    for p in range(len(pairs) - 1):
        at = 2 * cols * (p // 2)
        cells_ref[1 - p % 2, :, at : at + 2 * cols] = jnp.concatenate(pairs[p : p + 2], 0).T


def inner(own, tail, field):
    rows, cols, chans = own.shape
    width = cols + tail.shape[2]
    whole = pl.BlockSpec(memory_space=pltpu.VMEM)
    return pl.pallas_call(
        functools.partial(inner_kernel, field),
        out_shape=(
            jax.ShapeDtypeStruct((rows // 2, width, 6 * chans), BF16),
            jax.ShapeDtypeStruct((2, 6 * chans, cols * (rows // 2 - 2)), BF16),
        ),
        in_specs=[whole] * 2,
        out_specs=(whole, whole),
        compiler_params=pltpu.CompilerParams(vmem_limit_bytes=PREP_LIMIT),
        cost_estimate=pl.CostEstimate(flops=1 << 31, bytes_accessed=8 << 20, transcendentals=0),
    )(own, tail)


def outer_kernel(
    even_ref, odd_ref, feat_near_ref, cot_near_ref, taps_ref, cells_ref
):
    pairs = feat_near_ref.shape[0]
    chans = even_ref.shape[3]
    cols = cells_ref.shape[3] // 2
    odd = lax.axis_index("lat") % 2 == 1

    def whole(first_ref, second_ref, at):
        return jnp.where(odd, first_ref[at].astype(F32), second_ref[at].astype(F32)).astype(BF16)

    for field in range(2):

        def near(r):
            p, r = divmod(r % (2 * pairs), 2)
            at = [(2 * b + r) * chans for b in range(3)]
            near_ref = (feat_near_ref, cot_near_ref)[field]
            return [near_ref[p, :, i : i + chans] for i in at]

        above = [shifted(whole(even_ref, odd_ref, (field, r))) for r in range(2)]
        below = [shifted(whole(odd_ref, even_ref, (field, r))) for r in range(2)]
        taps_ref[field, 0] = paired(*above)
        taps_ref[field, 1] = paired(*below)
        cells = [paired(above[1], near(0)), paired(near(1), near(2))]
        cells_ref[field, 0] = jnp.concatenate([cell[:cols] for cell in cells], 0).T
        cells = [paired(near(-3), near(-2)), paired(near(-1), below[0])]
        cells_ref[field, 1] = jnp.concatenate([cell[:cols] for cell in cells], 0).T


def outer(rims, near, cols):
    _, _, width, chans = rims[0].shape
    whole = pl.BlockSpec(memory_space=pltpu.VMEM)
    return pl.pallas_call(
        outer_kernel,
        out_shape=(
            jax.ShapeDtypeStruct((2, 2, width, 6 * chans), BF16),
            jax.ShapeDtypeStruct((2, 2, 6 * chans, 2 * cols), BF16),
        ),
        in_specs=[whole] * 4,
        out_specs=(whole, whole),
        compiler_params=pltpu.CompilerParams(vmem_limit_bytes=PREP_LIMIT),
        cost_estimate=pl.CostEstimate(flops=1 << 30, bytes_accessed=4 << 20, transcendentals=0),
    )(*rims, *near)


def tap_rows(a, b, chans):
    tap = (a + 1) * 3 + b + 1
    return slice(tap * chans, (tap + 1) * chans)


def fill_plain(weight_ref, table_ref):
    chans = weight_ref.shape[1]
    for half in range(2):
        for b in range(3):
            for source in range(2):
                for target in range(2):
                    a = 2 * half + source - target - 1
                    at = (2 * b + source) * chans
                    if abs(a) <= 1:
                        block = weight_ref[tap_rows(a, b - 1, chans)]
                    else:
                        block = jnp.zeros((chans, chans), BF16)
                    table_ref[half, at : at + chans, target * chans : (target + 1) * chans] = block


def fill_turned(weight_ref, table_ref):
    chans = weight_ref.shape[1]
    for half in range(2):
        for b in range(3):
            for source in range(2):
                for target in range(2):
                    a = 2 * half + source - target - 1
                    at = (2 * b + source) * chans
                    if abs(a) <= 1:
                        block = weight_ref[tap_rows(-a, 1 - b, chans)]
                    else:
                        block = jnp.zeros((chans, chans), BF16)
                    table_ref[half, target * chans : (target + 1) * chans, at : at + chans] = block


def plain(lhs, rhs):
    return lax.dot_general(lhs, rhs, (((1,), (0,)), ((), ())), preferred_element_type=F32)


def turned(lhs, rhs):
    return lax.dot_general(lhs, rhs, (((1,), (1,)), ((), ())), preferred_element_type=F32)


def tables_kernel(
    own_rows, mine_ref, other_ref, one_ref, plain_ref, turned_ref, mixed_ref, wide_ref, two_ref
):
    taps = one_ref.shape[0]
    core = lax.axis_index(AXES) % 2
    mixed_ref[0] = mine_ref[...].astype(F32)
    mixed_ref[1] = other_ref[...].astype(F32)
    for g in range(mine_ref.shape[0] // own_rows):
        at = own_rows * g
        mine, other = (mixed_ref[i, at : at + own_rows] for i in range(2))
        wide_ref[2 * at : 2 * at + own_rows] = jnp.where(core == 0, mine, other)
        wide_ref[2 * at + own_rows : 2 * at + 2 * own_rows] = jnp.where(core == 0, other, mine)
    one_ref[...] = wide_ref[pl.ds(0, taps, stride=2)].astype(BF16)
    two_ref[...] = wide_ref[pl.ds(1, taps, stride=2)].astype(BF16)
    fill_plain(one_ref, plain_ref)
    fill_turned(two_ref, turned_ref)


def tables(both, own_rows):
    rows, chans = both[0].shape
    lanes = 2 * chans
    whole = pl.BlockSpec(memory_space=pltpu.VMEM)
    return pl.pallas_call(
        functools.partial(tables_kernel, own_rows),
        out_shape=(
            jax.ShapeDtypeStruct((rows, chans), BF16),
            jax.ShapeDtypeStruct((2, 3 * lanes, lanes), BF16),
            jax.ShapeDtypeStruct((2, lanes, 3 * lanes), BF16),
        ),
        in_specs=[whole] * 2,
        out_specs=(whole,) * 3,
        scratch_shapes=[
            pltpu.VMEM((2, rows, chans), F32),
            pltpu.VMEM((2 * rows, chans), F32),
            pltpu.VMEM((rows, chans), BF16),
        ],
        compiler_params=pltpu.CompilerParams(vmem_limit_bytes=PREP_LIMIT),
        cost_estimate=pl.CostEstimate(flops=1 << 30, bytes_accessed=4 << 20, transcendentals=0),
    )(*both)


def middle_kernel(
    own_rows, plain_ref, turned_ref, feat_taps_ref, cot_taps_ref, feat_cells_ref, cot_cells_ref, outer_taps_ref, outer_cells_ref,
    keep_ref, send_ref, back_ref,
    sums_ref, slope_ref, act_ref, own_ref,
):
    pairs, width, lanes = back_ref.shape
    chans = lanes // 2
    cols = width - 16
    core = lax.axis_index(AXES) % 2
    lat = lax.axis_index("lat")

    def rows_of(field, first, count):
        parts = []
        for p in range(first, first + count):
            if p == 0:
                parts.append(outer_taps_ref[field, 0])
            elif p == pairs:
                parts.append(outer_taps_ref[field, 1])
            else:
                parts.append((feat_taps_ref, cot_taps_ref)[field][p - 1])
        return jnp.concatenate(parts, 0)

    def cells_of(field, shift):
        parts = [outer_cells_ref[field, shift], (feat_cells_ref, cot_cells_ref)[field][shift]]
        return jnp.concatenate(parts if shift == 0 else parts[::-1], 1)

    lane = lax.broadcasted_iota(jnp.int32, (1, lanes), 1)
    step = pairs // 3
    for c in range(0, pairs, step):
        pre = plain(rows_of(0, c, step), plain_ref[0]) + plain(rows_of(0, c + 1, step), plain_ref[1])
        sigma = jax.nn.sigmoid(pre)
        act = (pre * sigma).astype(BF16)
        slope_ref[...] = sigma * (1.0 + pre * (1.0 - sigma))
        back = turned(rows_of(1, c, step), turned_ref[0]) + turned(
            rows_of(1, c + 1, step), turned_ref[1]
        )
        back = (back * slope_ref[...]).astype(BF16)
        for p in range(step):
            part = back[width * p : width * (p + 1)]
            for out_ref, rows in ((act_ref, act[width * p : width * p + cols]), (own_ref, part[:cols])):
                at = cols * (c + p)
                if c + p < pairs - 1:
                    out_ref[at : at + cols, :chans] = rows[:, chans:]
                if c + p > 0:
                    out_ref[at - cols : at, chans:] = rows[:, :chans]
            if c + p == 0:
                part = jnp.where((lane < chans) & (lat == 0), 0.0, part.astype(F32)).astype(BF16)
            if c + p == pairs - 1:
                part = jnp.where((lane >= chans) & (lat == lax.axis_size("lat") - 1), 0.0, part.astype(F32)).astype(BF16)
            back_ref[c + p] = part
    seconds = [plain(cells_of(1, d), act_ref[...]) for d in range(2)]
    firsts = [plain(cells_of(0, d), own_ref[...]) for d in range(2)]
    for a in range(-1, 2):
        for b in range(3):

            def summed(halves):
                total = None
                for half in range(2):
                    for source in range(2):
                        target = 2 * half + source - 1 - a
                        if target in (0, 1):
                            at = (2 * b + source) * chans
                            block = halves[half][at : at + chans, target * chans : (target + 1) * chans]
                            total = block if total is None else total + block
                return total

            at = tap_rows(a, b - 1, chans).start
            sums_ref[pl.ds(2 * at, chans, stride=2)] = summed(firsts)
            at = tap_rows(-a, 1 - b, chans).start
            sums_ref[pl.ds(2 * at + 1, chans, stride=2)] = summed(seconds).T
    groups = keep_ref.shape[0] // own_rows
    for g in range(groups):
        out = pl.ds(own_rows * g, own_rows)
        keep_ref[out] = sums_ref[pl.ds(own_rows * (2 * g + core), own_rows)]
        send_ref[out] = sums_ref[pl.ds(own_rows * (2 * g + 1 - core), own_rows)]


def middle(plain_table, turned_table, inner_parts, outer_parts, own_rows):
    inner_taps, inner_cells = inner_parts
    outer_taps, outer_cells = outer_parts
    pairs, width = inner_taps[0].shape[0] + 1, inner_taps[0].shape[1]
    lanes = plain_table.shape[2]
    chans = lanes // 2
    rows = 18 * chans
    cells = (pairs - 1) * (width - 16)
    whole = pl.BlockSpec(memory_space=pltpu.VMEM)
    return pl.pallas_call(
        functools.partial(middle_kernel, own_rows),
        out_shape=(
            jax.ShapeDtypeStruct((rows // 2, chans), F32),
            jax.ShapeDtypeStruct((rows // 2, chans), F32),
            jax.ShapeDtypeStruct((pairs, width, lanes), BF16),
        ),
        in_specs=[whole] * 8,
        out_specs=(whole,) * 3,
        scratch_shapes=[
            pltpu.VMEM((rows, chans), F32),
            pltpu.VMEM((pairs // 3 * width, lanes), F32),
            pltpu.VMEM((cells, lanes), BF16),
            pltpu.VMEM((cells, lanes), BF16),
        ],
        compiler_params=pltpu.CompilerParams(vmem_limit_bytes=MIDDLE_LIMIT),
    )(plain_table, turned_table, *inner_taps, *inner_cells, outer_taps, outer_cells)


def final_kernel(one_ref, back_ref, cot_ref, out_ref, turned_ref, taps_ref):
    pairs, _, _ = back_ref.shape
    _, cols, chans = cot_ref.shape
    fill_turned(one_ref, turned_ref)
    for p in range(pairs):
        taps = jnp.concatenate(shifted(back_ref[p]), 1)
        taps_ref[cols * p : cols * (p + 1)] = taps[:cols]
    step = (pairs - 1) // 2
    for c in range(0, pairs - 1, step):
        total = turned(taps_ref[cols * c : cols * (c + step)], turned_ref[0]) + turned(
            taps_ref[cols * (c + 1) : cols * (c + step + 1)], turned_ref[1]
        )
        for p in range(step):
            for r in range(2):
                row = 2 * (c + p) + r
                part = total[cols * p : cols * (p + 1), r * chans : (r + 1) * chans]
                out_ref[row] = (part + cot_ref[row].astype(F32)).astype(BF16)


def final(one, back, cotangent):
    pairs, _, lanes = back.shape
    _, cols, _ = cotangent.shape
    whole = pl.BlockSpec(memory_space=pltpu.VMEM)
    return pl.pallas_call(
        final_kernel,
        out_shape=jax.ShapeDtypeStruct(cotangent.shape, BF16),
        in_specs=[whole] * 3,
        out_specs=whole,
        scratch_shapes=[
            pltpu.VMEM((2, lanes, 3 * lanes), BF16),
            pltpu.VMEM((pairs * cols, 3 * lanes), BF16),
        ],
        compiler_params=pltpu.CompilerParams(vmem_limit_bytes=FINAL_LIMIT),
        cost_estimate=pl.CostEstimate(flops=1 << 32, bytes_accessed=8 << 20, transcendentals=0),
    )(one, back, cotangent)


def layer(features, cotangent, w_first, w_second):
    both = gather_kernels(w_first, w_second)
    rows, cols, chans = features.shape
    lon, lat = lax.axis_index("lon"), lax.axis_index("lat")

    def edge(field, axis, first):
        size = field.shape[axis]
        start = jnp.where(first, 0, size - 2)
        return lax.dynamic_slice_in_dim(field, start, 2, axis)

    def edges(axis, first):
        return jnp.stack([edge(features, axis, first), edge(cotangent, axis, first)])

    lat_odd, lon_odd = lat % 2 == 1, lon % 2 == 1
    rims, sides = [None, None], [None, None]
    for turn in (1, 0):
        sides[turn] = swap(edges(1, lon_odd ^ (turn == 1)), "lon", turn, True)
    right = jnp.where(lon_odd, sides[1], sides[0])
    left = jnp.where(lon_odd, sides[0], sides[1])
    tail = jnp.concatenate([right, jnp.zeros((2, rows, 12, chans), BF16), left], 2)
    for turn in (1, 0):
        first = lat_odd ^ (turn == 1)
        sent = jnp.concatenate([edges(0, first), edge(tail, 1, first)], 2)
        rims[turn] = swap(sent, "lat", turn, False)
    staged = stage(features)
    _, own_tail = lax.optimization_barrier((both[0], tail))
    parts = [inner(own, own_tail, field) for field, own in enumerate((staged, cotangent))]
    inner_parts = tuple(zip(*parts))
    one, plain_table, turned_table = tables(both, 2 * w_first.shape[0])
    rims, plain_table = lax.optimization_barrier((rims, plain_table))
    outer_parts = outer(rims, inner_parts[0], cols)
    keep, send, back = middle(plain_table, turned_table, inner_parts, outer_parts, 2 * w_first.shape[0])
    grads = scatter_sums(keep, send)
    return final(one, back, cotangent), *grads


def solution(mesh):
    in_specs = (
        P("lat", "lon", None),
        P("lat", "lon", None),
        P(("lat", "lon"), None),
        P(("lat", "lon"), None),
    )
    out_specs = (P("lat", "lon", None), P(("lat", "lon"), None), P(("lat", "lon"), None))
    return jax.shard_map(layer, mesh=mesh, in_specs=in_specs, out_specs=out_specs, check_vma=False)
```
